32 devices in a mesh: sub: 2 (over x), row: 4 (over y, core), col: 4 (over z).
Axes of the slice: x: 2, y: 2, z: 4, core: 2. Of those that a mesh axis runs over, the one named last changes fastest.
Arguments:
- child_update: float32 [2, 4096, 4096], P('sub', 'row', 'col'), as said below
- child_coupling: bfloat16 [2, 4096, 2048], P('sub', 'row', 'col'), may hold values from -0.0625 to 0.0625
- pivot_inverse: bfloat16 [2, 2048, 2048], P('sub', 'col'), as said below
- child_map: int32 [2, 16], replicated, may hold values from 0 to 31, as said below
- parent_front: float32 [8192, 8192], P(('sub', 'row'), 'col'), as said below
- block_pattern: int32 [32, 32], P(('sub', 'row'), 'col'), may hold values from 0 to 1, as said below
Outputs:
- factored: float32 [8192, 8192], P(('sub', 'row'), 'col')
The draws below stay inside these ranges and needn't reach their ends.
Inputs may be any that keep to these rules, and one draw needn't show every extreme that they name: child_map[s, b] is the parent block that block b of child s lands in, for rows and columns alike; one child's values are distinct, and child_map[s, b] // 8 == b // 4. `block_pattern`: Symmetric, with ones on the diagonal and in every block row and block column below 2. `child_update`: each child's matrix is symmetric. `parent_front`: Symmetric. `pivot_inverse`: each child's matrix is lower triangular with a nonzero diagonal.
All inputs are finite; a program needn't handle non-finite values.
Results may differ from the reference program's by a relative error of at most 0.0019.
Values may be sent and summed in bfloat16 or wider, within the bound.
No kernel may reach another device: no remote copies, remote signals or barrier semaphores. Data moves between devices by JAX's collectives and lax.ppermute only.
A program may use at most 128 MiB of HBM per device.

```python
import math
import jax
import jax.numpy as jnp
from jax import lax

BLK = 256
KC = 2048
MC = 4096
FP = 8192
PSTEPS = 2
NBC = 16
NBP = 32
CB = 4
CBP = 8
KP = 512


def draw_child_update(key, part):
    noise_key, diag_key, basis_key = jax.random.split(jax.random.fold_in(key, 11), 3)
    basis_width = 2 * BLK
    noise_draw = jnp.clip(jax.random.normal(noise_key, (2, MC, MC), jnp.float32), -6.0, 6.0)
    basis_draw = jnp.clip(jax.random.normal(basis_key, (2, MC, basis_width), jnp.float32), -6.0, 6.0)
    diagonal = jax.random.uniform(diag_key, (2, MC), jnp.float32, 3.0, 4.0)
    symmetric = (noise_draw + jnp.swapaxes(noise_draw, 1, 2)) * (0.05 / math.sqrt(2.0 * MC))
    scaled_basis = basis_draw * math.sqrt(3.0 / basis_width)
    gram_part = jnp.einsum('smr,snr->smn', scaled_basis, scaled_basis, precision=lax.Precision.HIGHEST)
    diag_index = jnp.arange(MC)
    return (gram_part + symmetric).at[:, diag_index, diag_index].add(diagonal)


def draw_pivot_inverse(key, part):
    noise_key, diag_key = jax.random.split(jax.random.fold_in(key, 23))
    noise_draw = jnp.clip(jax.random.normal(noise_key, (2, KC, KC), jnp.float32), -6.0, 6.0)
    diagonal = jax.random.uniform(diag_key, (2, KC), jnp.float32, 0.8, 1.25)
    strict_lower = jnp.tril(noise_draw, -1) * (1.0 / math.sqrt(KC))
    diag_index = jnp.arange(KC)
    return strict_lower.at[:, diag_index, diag_index].set(diagonal).astype(jnp.bfloat16)


def pin_first(ordering, value):
    swapped = jnp.where(ordering == value, ordering[0], ordering)
    return swapped.at[0].set(value)


def draw_child_map(key, part):
    groups = NBC // CB
    key_list = jax.random.split(jax.random.fold_in(key, 37), 2 * groups)
    orders = jax.vmap(lambda subkey: jax.random.permutation(subkey, CBP))(key_list)
    orders = orders.at[0].set(pin_first(orders[0], 0))
    orders = orders.at[2 * groups - 1].set(pin_first(orders[2 * groups - 1], CBP - 1))
    offsets = jnp.arange(2 * groups, dtype=jnp.int32) % groups * CBP
    return (orders[:, :CB] + offsets[:, None]).reshape(2, NBC).astype(jnp.int32)


def draw_parent_front(key, part):
    noise_key, diag_key = jax.random.split(jax.random.fold_in(key, 41))
    noise_draw = jnp.clip(jax.random.normal(noise_key, (FP, FP), jnp.float32), -6.0, 6.0)
    diagonal = jax.random.uniform(diag_key, (FP,), jnp.float32, 1.0, 1.5)
    symmetric = (noise_draw + noise_draw.T) * (1.0 / math.sqrt(2.0 * FP))
    diag_index = jnp.arange(FP)
    return symmetric.at[diag_index, diag_index].add(diagonal)


def draw_block_pattern(key, part):
    bits_draw = jax.random.randint(jax.random.fold_in(key, 53), (NBP, NBP), 0, 2, jnp.int32)
    strict_lower = jnp.tril(bits_draw, -1)
    pattern = strict_lower + strict_lower.T + jnp.eye(NBP, dtype=jnp.int32)
    leading = jnp.arange(NBP, dtype=jnp.int32) < PSTEPS
    dense_part = leading[:, None] | leading[None, :]
    return jnp.where(dense_part, jnp.int32(1), pattern).astype(jnp.int32)


def steps_of(key, dims, shards, least, top_value):
    factor_of = 1.0
    for position, parts in shards:
        heights = jax.random.uniform(jax.random.fold_in(jax.random.fold_in(key, 6), position), (parts,), jnp.float32, least / len(shards), top_value / len(shards))
        factor_of = factor_of * jnp.repeat(jnp.exp(heights), dims[position] // parts).reshape((-1,) + (1,) * (len(dims) - 1 - position))
    return factor_of


def noise(stream_key, extent, deviation, limit, cuts=(), kind=jnp.bfloat16):
    values = deviation * jax.random.normal(stream_key, extent, jnp.float32)
    if cuts:
        values = values * steps_of(stream_key, extent, cuts, -0.22, 0.18)
    return jnp.clip(values, -limit, limit).astype(kind)


def setup_inputs(seed: int = 0) -> dict:
    arg_keys = jax.random.split(jax.random.key(seed), 7)
    child_update = draw_child_update(jax.random.fold_in(arg_keys[6], 71), 0)
    child_coupling = noise(arg_keys[1], (2, MC, KC), (4 * KC) ** -0.5, 0.0625, ((0, 2), (1, 4), (2, 4)))
    pivot_inverse = draw_pivot_inverse(jax.random.fold_in(arg_keys[6], 71), 0)
    child_map = draw_child_map(jax.random.fold_in(arg_keys[6], 71), 0)
    parent_front = draw_parent_front(jax.random.fold_in(arg_keys[6], 71), 0)
    block_pattern = draw_block_pattern(jax.random.fold_in(arg_keys[6], 71), 0)
    return {"child_update": child_update, "child_coupling": child_coupling, "pivot_inverse": pivot_inverse, "child_map": child_map, "parent_front": parent_front, "block_pattern": block_pattern}


def reference(child_update, child_coupling, pivot_inverse, child_map, parent_front, block_pattern):
    pattern = block_pattern.astype(jnp.float32)
    assembled = parent_front.reshape(NBP, BLK, NBP, BLK) * pattern[:, None, :, None]
    for child_index in range(2):
        child_panel = jnp.dot(child_coupling[child_index].astype(jnp.float32), pivot_inverse[child_index].T.astype(jnp.float32), preferred_element_type=jnp.float32).astype(jnp.bfloat16)
        schur_part = child_update[child_index] - jnp.dot(child_panel.astype(jnp.float32), child_panel.T.astype(jnp.float32), preferred_element_type=jnp.float32)
        blocks = schur_part.reshape(NBC, BLK, NBC, BLK).transpose(0, 2, 1, 3)
        mapping = child_map[child_index]
        assembled = assembled.at[mapping[:, None], :, mapping[None, :], :].add(blocks)
    assembled = assembled.reshape(FP, FP)
    identity = jnp.eye(BLK, dtype=jnp.float32)
    for step_index in range(PSTEPS):
        edge_low = step_index * BLK
        edge_high = edge_low + BLK
        lower_pivot = jnp.linalg.cholesky(assembled[edge_low:edge_high, edge_low:edge_high])
        inverse = jax.scipy.linalg.solve_triangular(lower_pivot, identity, lower=True)
        below_rows = jnp.dot(assembled[edge_high:, edge_low:edge_high], inverse.T, precision=lax.Precision.HIGHEST)
        assembled = assembled.at[edge_high:, edge_high:].add(-jnp.dot(below_rows, below_rows.T, precision=lax.Precision.HIGHEST))
        assembled = assembled.at[edge_low:edge_high, edge_low:edge_high].set(lower_pivot)
        assembled = assembled.at[edge_high:, edge_low:edge_high].set(below_rows)
    row_ids = jnp.arange(FP, dtype=jnp.int32)[:, None]
    col_ids = jnp.arange(FP, dtype=jnp.int32)[None, :]
    return jnp.where((row_ids < KP) & (col_ids > row_ids), jnp.float32(0.0), assembled)
```

```python
import jax
import jax.numpy as jnp
from jax import lax
from jax.experimental import pallas as pl
from jax.experimental.pallas import tpu as pltpu
from jax.sharding import PartitionSpec as P

BLK = 256
PSTEPS = 2
KP = PSTEPS * BLK
TILE = 128
PLANE = ("sub", "row")


highest = lax.Precision.HIGHEST
high = lax.Precision.HIGH


def nt(a, b, precision=None):
    return lax.dot_general(
        a, b, (((1,), (1,)), ((), ())), precision=precision, preferred_element_type=jnp.float32
    )


def nn(a, b, precision=None):
    return lax.dot_general(
        a, b, (((1,), (0,)), ((), ())), precision=precision, preferred_element_type=jnp.float32
    )


def line_gather(own):
    n = lax.axis_size("col")
    ups, downs = [own], [own]
    for t in range(1, n):
        ups.append(lax.ppermute(ups[-1], "col", [(i, i + 1) for i in range(t - 1, n - 1)]))
        downs.append(lax.ppermute(downs[-1], "col", [(i + 1, i) for i in range(n - t)]))
    return [own] + [ups[m] + downs[n - m] for m in range(1, n)]


def line_spread(x, chunks):
    n = lax.axis_size("col")
    first = lax.axis_index("col") == 0
    step = x.shape[0] // chunks
    done = []
    for c in range(chunks):
        part = x[c * step : (c + 1) * step]
        moving, total = part, jnp.where(first, part, jnp.zeros_like(part))
        for t in range(n - 1):
            moving = lax.ppermute(moving, "col", [(t, t + 1)])
            total = total + moving
        done.append(total)
    return done


def row_spread(x, root):
    rows, n = lax.axis_size("row"), lax.axis_size("col")
    away = lax.axis_index("row") ^ root(lax.axis_index("col"))
    bits = [1 << b for b in range(1, rows.bit_length() - 1)] + [1]
    done = 0
    for bit in bits:
        pairs = []
        for c in range(n):
            for d in range(rows):
                if d & ~done == 0:
                    src = root(c) ^ d
                    pairs.append((src * n + c, (src ^ bit) * n + c))
        got = lax.ppermute(x, ("row", "col"), pairs)
        x = jnp.where((away & ~done) == 0, x, got)
        done |= bit
    return x


def row_collect(x):
    rows = lax.axis_size("row")
    for bit in [1 << b for b in range(1, rows.bit_length() - 1)] + [1]:
        got = lax.ppermute(x, "row", [(i, i ^ bit) for i in range(rows)])
        x = jnp.concatenate([x, got], axis=0)
    return x


def plane_spread(x, here):
    rows, subs = lax.axis_size("row"), lax.axis_size("sub")
    across = [rows << b for b in range(subs.bit_length() - 1)]
    along = [1 << b for b in range(1, rows.bit_length() - 1)]
    half = x.shape[0] // 2
    out = []
    for part, bits in ((x[:half], along + across + [1]), (x[half:], across + along + [1])):
        done = 0
        for bit in bits:
            pairs = [(d, d ^ bit) for d in range(rows * subs) if d & ~done == 0]
            got = lax.ppermute(part, PLANE, pairs)
            part = jnp.where((here & ~done) == 0, part, got)
            done |= bit
        out.append(part)
    return jnp.concatenate(out, axis=0)


def pack(x):
    top = jnp.max(jnp.abs(x))
    top = jnp.where(top > 0, top, 1.0)
    return (x * (1.0 / top)).astype(jnp.float16), jnp.full((8, 128), top, jnp.float32)


def eliminate(block):
    t = block.shape[0]
    lane = lax.broadcasted_iota(jnp.int32, (8, t), 1)
    sub = lax.broadcasted_iota(jnp.int32, (8, t), 0)
    rows = [block[8 * i : 8 * i + 8] for i in range(t // 8)]
    inverse = [jnp.where(lane == sub + 8 * i, 1.0, 0.0) for i in range(t // 8)]
    for j in range(t - 1):
        q, p = divmod(j, 8)
        lead, lead_inverse = rows[q][p : p + 1], inverse[q][p : p + 1]
        scale = 1.0 / jnp.broadcast_to(lead[:, j : j + 1], (1, t))
        lead = jnp.broadcast_to(lead * scale, (8, t))
        lead_inverse = jnp.broadcast_to(lead_inverse * scale, (8, t))
        for i in range(q, t // 8):
            if i == q and p == 7:
                continue
            factor = jnp.broadcast_to(rows[i][:, j : j + 1], (8, t))
            if i == q:
                factor = jnp.where(sub > p, factor, 0.0)
            rows[i] = rows[i] - factor * lead
            inverse[i] = inverse[i] - factor * lead_inverse
    return jnp.concatenate(rows, 0), jnp.concatenate(inverse, 0)


def factor_kernel(a_ref, lower_ref, inverse_ref, work_ref):
    size = a_ref.shape[0]
    work_ref[...] = a_ref[...]
    lower_ref[...] = jnp.zeros_like(lower_ref)
    inverse_ref[...] = jnp.zeros_like(inverse_ref)
    r = lax.broadcasted_iota(jnp.int32, (TILE, TILE), 0)
    c = lax.broadcasted_iota(jnp.int32, (TILE, TILE), 1)

    def step(b, carry):
        at = pl.multiple_of(b * TILE, TILE)
        here = pl.ds(at, TILE)
        upper, unit = eliminate(work_ref[here, here])
        pivots = jnp.sum(jnp.where(r == c, upper, 0.0), axis=1, keepdims=True)
        root = 1.0 / jnp.sqrt(pivots)
        diagonal = jnp.where(c >= r, upper * root, 0.0).T
        local = unit * root
        column = nt(work_ref[:, here], local, highest)
        ids = lax.broadcasted_iota(jnp.int32, (size, TILE), 0)
        column = jnp.where(ids >= at + TILE, column, 0.0)
        work_ref[...] = work_ref[...] - nt(column, column, highest)
        known = nn(lower_ref[here, :], inverse_ref[...], highest)
        rr = lax.broadcasted_iota(jnp.int32, (TILE, size), 0)
        cc = lax.broadcasted_iota(jnp.int32, (TILE, size), 1)
        inverse_ref[here, :] = nn(local, jnp.where(cc == rr + at, 1.0, 0.0) - known, highest)
        lower_ref[:, here] = column
        lower_ref[here, here] = diagonal
        return carry

    lax.fori_loop(0, size // TILE, step, 0)


def factor_pivot(block):
    return pl.pallas_call(
        factor_kernel,
        out_shape=[jax.ShapeDtypeStruct(block.shape, jnp.float32)] * 2,
        scratch_shapes=[pltpu.VMEM(block.shape, jnp.float32)],
        name="factor_pivot",
    )(block)


def assemble_kernel(where_ref, pattern_ref, parent_ref, first_ref, second_ref, out_ref):
    i = pl.program_id(0)
    group_cols = parent_ref.shape[1] // BLK
    group_rows = pl.num_programs(0)
    for k in range(group_cols):
        cols = slice(k * BLK, (k + 1) * BLK)
        value = parent_ref[:, cols] * pattern_ref[i, k].astype(jnp.float32)
        for s, ref in enumerate((first_ref, second_ref)):
            source = where_ref[s, group_rows + k]
            hit = jnp.logical_and(where_ref[s, i] >= 0, source >= 0)
            block = ref[:, pl.ds(pl.multiple_of(jnp.maximum(source, 0) * BLK, BLK), BLK)]
            value = value + jnp.where(hit, block, 0.0)
        out_ref[:, cols] = value


def assemble(places, pattern, parent, first, second):
    rows, cols = parent.shape
    width = first.shape[1]

    def source(s):
        return pl.BlockSpec((BLK, width), lambda i, w, p: (jnp.maximum(w[s, i], 0), 0))

    return pl.pallas_call(
        assemble_kernel,
        out_shape=jax.ShapeDtypeStruct(parent.shape, jnp.float32),
        grid_spec=pltpu.PrefetchScalarGridSpec(
            num_scalar_prefetch=2,
            grid=(rows // BLK,),
            in_specs=[pl.BlockSpec((BLK, cols), lambda i, w, p: (i, 0)), source(0), source(1)],
            out_specs=pl.BlockSpec((BLK, cols), lambda i, w, p: (i, 0)),
        ),
        name="assemble",
    )(places, pattern, parent, first, second)


def local(child_update, child_coupling, pivot_inverse, child_map, parent_front, block_pattern):
    update, coupling, inverse_rows = child_update[0], child_coupling[0], pivot_inverse[0]
    rows, width = update.shape
    depth = coupling.shape[1]
    full_depth = inverse_rows.shape[1]
    n, ranks = lax.axis_size("col"), lax.axis_size("row")
    col, row, sub = lax.axis_index("col"), lax.axis_index("row"), lax.axis_index("sub")
    here = sub * ranks + row
    local_rows, local_cols = parent_front.shape

    owner = lambda c: c * width // rows
    blocks = line_gather(coupling)
    pieces = []
    for block in blocks:
        slab = block
        if width != rows:
            slab = lax.dynamic_slice_in_dim(block, col * width - owner(col) * rows, width, 0)
        pieces.append(jnp.concatenate([block, row_spread(slab, owner)], axis=0))
    both = jnp.zeros((rows + width, full_depth), coupling.dtype)
    for m, piece in enumerate(pieces):
        both = lax.dynamic_update_slice(both, piece, (0, (col - m) % n * depth))

    share = inverse_rows.shape[0] // ranks
    mine = lax.dynamic_slice_in_dim(inverse_rows, row * share, share, 0)
    panels = [nt(both, row_collect(part)).astype(jnp.bfloat16) for part in line_gather(mine)]
    panel = jnp.concatenate(panels, axis=1)
    schur = update - nt(panel[:rows], panel[rows:])

    packed, top = pack(schur)
    half = rows // 2
    is_first = sub == 0
    straight = [(s * ranks + r, 2 * r + s) for s in range(2) for r in range(ranks)]
    crossed = [(s * ranks + r, 2 * r + 1 - s) for s in range(2) for r in range(ranks)]
    swap = [(i, i ^ 1) for i in range(2 * ranks)]

    def route(value, cut):
        a, b = (value[:cut], value[cut:]) if cut else (value, value)
        got = lax.ppermute(jnp.where(is_first, a, b), PLANE, straight)
        other = lax.ppermute(jnp.where(is_first, b, a), PLANE, crossed)
        even = here % 2 == 0
        return jnp.where(even, got, other), jnp.where(even, other, got)

    tops = route(top, 0)
    halves = route(packed, half)
    partner = [lax.ppermute(h, PLANE, swap) for h in halves]
    even = here % 2 == 0
    whole = []
    for s in range(2):
        scale = tops[s][0, 0]
        low = jnp.where(even, halves[s], partner[s])
        top_half = jnp.where(even, partner[s], halves[s])
        whole.append(jnp.concatenate([low, top_half], axis=0).astype(jnp.float32) * scale)

    group_rows, group_cols = local_rows // BLK, local_cols // BLK
    child_rows, child_cols = rows // BLK, width // BLK

    def place(first, count, targets):
        inside = lax.dynamic_slice_in_dim(child_map, first, count, 1)
        match = inside[:, None, :] == targets[None, :, None]
        return jnp.where(match.any(-1), jnp.argmax(match, axis=-1), -1).astype(jnp.int32)

    places = jnp.concatenate(
        [
            place(here // 2 * child_rows, child_rows, here * group_rows + jnp.arange(group_rows)),
            place(col * child_cols, child_cols, col * group_cols + jnp.arange(group_cols)),
        ],
        axis=1,
    )
    current = assemble(places, block_pattern, parent_front, whole[0], whole[1])

    first_col = col == 0
    lead_packed, lead_top = pack(current[:, :KP])
    parts = line_spread(lead_packed, local_rows // KP)
    lead_scale = line_spread(lead_top, 1)[0]
    pivot_scale = plane_spread(lead_scale, here)[0, 0]
    pivot = plane_spread(parts[0], here).astype(jnp.float32) * pivot_scale
    lower, inverse = factor_pivot(pivot)
    raw_packed, raw_top = pack(current[:KP])
    raw = plane_spread(raw_packed, here).astype(jnp.float32)
    raw = raw * plane_spread(raw_top, here)[0, 0]
    lead = jnp.concatenate(parts, axis=0).astype(jnp.float32) * lead_scale[0, 0]
    lead = jnp.where(first_col, current[:, :KP], lead)
    global_rows = here * local_rows + jnp.arange(local_rows, dtype=jnp.int32)
    global_cols = col * local_cols + jnp.arange(local_cols, dtype=jnp.int32)
    below = jnp.where((global_rows >= KP)[:, None], nt(lead, inverse, high), 0.0)
    current = current - nn(below, nn(inverse, raw, high), high)
    edge = jnp.concatenate([lower, jnp.zeros((local_rows - KP, KP), jnp.float32)], axis=0)
    edge = jnp.where((global_rows < KP)[:, None], edge, below)
    merged = jnp.where(first_col, edge, current[:, :KP])
    current = lax.dynamic_update_slice(current, merged, (0, 0))
    upper_mask = (global_rows[:, None] < KP) & (global_cols[None, :] > global_rows[:, None])
    return jnp.where(upper_mask, 0.0, current)


def solution(mesh):
    return jax.shard_map(
        local,
        mesh=mesh,
        in_specs=(
            P("sub", "row", "col"),
            P("sub", "row", "col"),
            P("sub", "col", None),
            P(),
            P(PLANE, "col"),
            P(PLANE, "col"),
        ),
        out_specs=P(PLANE, "col"),
        check_vma=False,
    )
```

```python
import functools

import jax
import jax.numpy as jnp
from jax import lax
from jax.experimental import pallas as pl
from jax.experimental.pallas import tpu as pltpu
from jax.sharding import PartitionSpec as P

BLK = 256
PSTEPS = 2
KP = PSTEPS * BLK
TILE = 128
PLANE = ("sub", "row")


high = lax.Precision.HIGH


def nt(a, b, precision=None):
    return lax.dot_general(
        a, b, (((1,), (1,)), ((), ())), precision=precision, preferred_element_type=jnp.float32
    )


def nn(a, b, precision=None):
    return lax.dot_general(
        a, b, (((1,), (0,)), ((), ())), precision=precision, preferred_element_type=jnp.float32
    )


def line_gather(own):
    n = lax.axis_size("col")
    ups, downs = [own], [own]
    for t in range(1, n):
        ups.append(lax.ppermute(ups[-1], "col", [(i, i + 1) for i in range(t - 1, n - 1)]))
        downs.append(lax.ppermute(downs[-1], "col", [(i + 1, i) for i in range(n - t)]))
    return [own] + [ups[m] + downs[n - m] for m in range(1, n)]


def tree_spread(x):
    n = lax.axis_size("col")
    col = lax.axis_index("col")
    step = n // 2
    while step:
        got = lax.ppermute(x, "col", [(i, i + step) for i in range(0, n, 2 * step)])
        x = jnp.where(col & (2 * step - 1) == step, got, x)
        step //= 2
    return x


def direct_spread(x):
    n = lax.axis_size("col")
    total = jnp.where(lax.axis_index("col") == 0, x, jnp.zeros_like(x))
    for t in range(1, n):
        total = total + lax.ppermute(x, "col", [(0, t)])
    return total


def row_spread(x, root):
    rows, n = lax.axis_size("row"), lax.axis_size("col")
    away = lax.axis_index("row") ^ root(lax.axis_index("col"))
    bits = [1 << b for b in range(1, rows.bit_length() - 1)] + [1]
    done = 0
    for bit in bits:
        pairs = []
        for c in range(n):
            for d in range(rows):
                if d & ~done == 0:
                    src = root(c) ^ d
                    pairs.append((src * n + c, (src ^ bit) * n + c))
        got = lax.ppermute(x, ("row", "col"), pairs)
        x = jnp.where((away & ~done) == 0, x, got)
        done |= bit
    return x


def row_collect(x):
    rows = lax.axis_size("row")
    for bit in [1 << b for b in range(1, rows.bit_length() - 1)] + [1]:
        got = lax.ppermute(x, "row", [(i, i ^ bit) for i in range(rows)])
        x = jnp.concatenate([x, got], axis=0)
    return x


def plane_spread(x, here):
    rows, subs = lax.axis_size("row"), lax.axis_size("sub")
    across = [rows << b for b in range(subs.bit_length() - 1)]
    along = [1 << b for b in range(1, rows.bit_length() - 1)]
    half = x.shape[0] // 2
    out = []
    for part, bits in ((x[:half], along + across + [1]), (x[half:], across + along + [1])):
        done = 0
        for bit in bits:
            pairs = [(d, d ^ bit) for d in range(rows * subs) if d & ~done == 0]
            got = lax.ppermute(part, PLANE, pairs)
            part = jnp.where((here & ~done) == 0, part, got)
            done |= bit
        out.append(part)
    return jnp.concatenate(out, axis=0)


def pack(x, power=None):
    if power is None:
        top = jnp.maximum(jnp.max(jnp.abs(x)), 1e-30)
        power = jnp.ceil(jnp.log2(top))
    body = (x * jnp.exp2(-power)).astype(jnp.float16)
    return jnp.concatenate([body, jnp.full((16, x.shape[1]), power, jnp.float16)], axis=0)


def power_of(packed):
    return packed[-1, -1].astype(jnp.float32)


def unpack(packed):
    return packed[:-16].astype(jnp.float32) * jnp.exp2(power_of(packed))


def split(x):
    top = x.astype(jnp.bfloat16)
    return top, (x - top.astype(jnp.float32)).astype(jnp.bfloat16)


def product(a, b, form):
    (a0, a1), (b0, b1) = split(a), split(b)
    return form(a0, b0) + (form(a0, b1) + form(a1, b0))


def eliminate(block):
    t = block.shape[0]
    lane = lax.broadcasted_iota(jnp.int32, (8, t), 1)
    sub = lax.broadcasted_iota(jnp.int32, (8, t), 0)
    rows = [block[8 * i : 8 * i + 8] for i in range(t // 8)]
    inverse = [jnp.where(lane == sub + 8 * i, 1.0, 0.0) for i in range(t // 8)]

    def wide(x):
        return jnp.broadcast_to(x, (8, t))

    for j in range(0, t, 2):
        q, p = divmod(j, 8)
        r1, r2 = wide(rows[q][p : p + 1]), wide(rows[q][p + 1 : p + 2])
        e1, e2 = wide(inverse[q][p : p + 1]), wide(inverse[q][p + 1 : p + 2])
        a, b, c = wide(r1[:, j : j + 1]), wide(r1[:, j + 1 : j + 2]), wide(r2[:, j + 1 : j + 2])
        over = 1.0 / a
        ratio = b * over
        under = 1.0 / (c - b * ratio)
        r2, e2 = r2 - ratio * r1, e2 - ratio * e1
        r1, e1, r2, e2 = r1 * over, e1 * over, r2 * under, e2 * under
        for i in range(q, t // 8):
            f1 = wide(rows[i][:, j : j + 1])
            f2 = wide(rows[i][:, j + 1 : j + 2]) - f1 * ratio
            if i == q:
                f1 = jnp.where(sub > p, f1, 0.0)
                f2 = jnp.where(sub > p + 1, f2, 0.0)
            rows[i] = rows[i] - f1 * r1 - f2 * r2
            inverse[i] = inverse[i] - f1 * e1 - f2 * e2
    return jnp.concatenate(rows, 0), jnp.concatenate(inverse, 0)


def factor_kernel(first, last, *refs):
    work_ref, lower_ref, inverse_ref = refs[-3:]
    size = work_ref.shape[0]
    if first == 0:
        work_ref[...] = refs[0][...]
        lower_ref[...] = jnp.zeros_like(lower_ref)
        inverse_ref[...] = jnp.zeros_like(inverse_ref)
    else:
        for source, target in zip(refs[:3], refs[3:]):
            target[...] = source[...]
    r = lax.broadcasted_iota(jnp.int32, (TILE, TILE), 0)
    c = lax.broadcasted_iota(jnp.int32, (TILE, TILE), 1)

    def step(b, carry):
        at = pl.multiple_of(b * TILE, TILE)
        here = pl.ds(at, TILE)
        upper, unit = eliminate(work_ref[here, here])
        pivots = jnp.sum(jnp.where(r == c, upper, 0.0), axis=1, keepdims=True)
        root = 1.0 / jnp.sqrt(pivots)
        diagonal = jnp.where(c >= r, upper * root, 0.0).T
        local = unit * root
        column = product(work_ref[:, here], local, nt)
        ids = lax.broadcasted_iota(jnp.int32, (size, TILE), 0)
        column = jnp.where(ids >= at + TILE, column, 0.0)
        work_ref[...] = work_ref[...] - product(column, column, nt)
        known = product(lower_ref[here, :], inverse_ref[...], nn)
        rr = lax.broadcasted_iota(jnp.int32, (TILE, size), 0)
        cc = lax.broadcasted_iota(jnp.int32, (TILE, size), 1)
        inverse_ref[here, :] = product(local, jnp.where(cc == rr + at, 1.0, 0.0) - known, nn)
        lower_ref[:, here] = column
        lower_ref[here, here] = diagonal
        return carry

    lax.fori_loop(first, last, step, 0)


def factor_steps(state, first, last):
    shape = jax.ShapeDtypeStruct(state[0].shape, jnp.float32)
    return pl.pallas_call(
        functools.partial(factor_kernel, first, last),
        out_shape=[shape] * 3,
        cost_estimate=pl.CostEstimate(
            flops=(last - first) * 10**10, transcendentals=0, bytes_accessed=3 * 2**21
        ),
        name="factor_pivot",
    )(*state)


def assemble_kernel(where_ref, pattern_ref, parent_ref, *refs):
    out_ref = refs[-1]
    i = pl.program_id(0)
    group_cols = parent_ref.shape[1] // BLK
    group_rows = pl.num_programs(0)
    for k in range(group_cols):
        cols = slice(k * BLK, (k + 1) * BLK)
        value = parent_ref[:, cols] * pattern_ref[i, k].astype(jnp.float32)
        for s, ref in enumerate(refs[:-1]):
            source = where_ref[s, group_rows + k]
            hit = jnp.logical_and(where_ref[s, i] >= 0, source >= 0)
            block = ref[:, pl.ds(pl.multiple_of(jnp.maximum(source, 0) * BLK, BLK), BLK)]
            value = value + jnp.where(hit, block, 0.0)
        out_ref[:, cols] = value


def assemble(places, pattern, parent, *children):
    rows, cols = parent.shape

    def source(s):
        shape = (BLK, children[s].shape[1])
        return pl.BlockSpec(shape, lambda i, w, p: (jnp.maximum(w[s, i], 0), 0))

    return pl.pallas_call(
        assemble_kernel,
        out_shape=jax.ShapeDtypeStruct(parent.shape, jnp.float32),
        grid_spec=pltpu.PrefetchScalarGridSpec(
            num_scalar_prefetch=2,
            grid=(rows // BLK,),
            in_specs=[pl.BlockSpec((BLK, cols), lambda i, w, p: (i, 0))]
            + [source(s) for s in range(len(children))],
            out_specs=pl.BlockSpec((BLK, cols), lambda i, w, p: (i, 0)),
        ),
        name="assemble",
    )(places, pattern, parent, *children)


def local(child_update, child_coupling, pivot_inverse, child_map, parent_front, block_pattern):
    update, coupling, inverse_rows = child_update[0], child_coupling[0], pivot_inverse[0]
    rows, width = update.shape
    depth = coupling.shape[1]
    full_depth = inverse_rows.shape[1]
    n, ranks = lax.axis_size("col"), lax.axis_size("row")
    col, row, sub = lax.axis_index("col"), lax.axis_index("row"), lax.axis_index("sub")
    here = sub * ranks + row
    local_rows, local_cols = parent_front.shape

    shift = (rows // width).bit_length() - 1
    owner = lambda c: c >> shift
    blocks = line_gather(coupling)
    pieces = []
    for block in blocks:
        slab = block
        if width != rows:
            slab = lax.dynamic_slice_in_dim(block, col * width - owner(col) * rows, width, 0)
        pieces.append(jnp.concatenate([block, row_spread(slab, owner)], axis=0))
    both = jnp.zeros((rows + width, full_depth), coupling.dtype)
    for m, piece in enumerate(pieces):
        both = lax.dynamic_update_slice(both, piece, (0, jnp.where(col >= m, col - m, col - m + n) * depth))

    share = inverse_rows.shape[0] // ranks
    mine = lax.dynamic_slice_in_dim(inverse_rows, row * share, share, 0)
    panels = [nt(both, row_collect(part)).astype(jnp.bfloat16) for part in line_gather(mine)]
    panel = jnp.concatenate(panels, axis=1)
    schur = update - nt(panel[:rows], panel[rows:])

    group_rows, group_cols = local_rows // BLK, local_cols // BLK
    child_rows, child_cols = rows // BLK, width // BLK

    def place(first, count, targets):
        inside = lax.dynamic_slice_in_dim(child_map, first, count, 1)
        match = inside[:, None, :] == targets[None, :, None]
        return jnp.where(match.any(-1), jnp.argmax(match, axis=-1), -1).astype(jnp.int32)

    pivots = jnp.arange(PSTEPS)
    pivot_places = lax.dynamic_slice_in_dim(
        jnp.concatenate([place(0, child_rows, pivots), place(0, child_cols, pivots)], axis=1),
        sub, 1, 0,
    )
    base = jnp.where(here == 0, parent_front[:KP, :KP], 0.0)
    ones = jnp.where(here == 0, block_pattern[:PSTEPS, :PSTEPS], 1)
    pivot = direct_spread(pack(assemble(pivot_places, ones, base, schur)))
    got = lax.ppermute(pivot, PLANE, [(0, ranks), (ranks, 0)])
    power = jnp.maximum(power_of(pivot), power_of(got)) + 1
    pivot = pack(unpack(pivot) + unpack(got), power)
    done = 0
    for bit in [1 << b for b in range(1, ranks.bit_length() - 1)] + [1]:
        pairs = [
            (s * ranks + d, s * ranks + (d ^ bit))
            for s in range(2) for d in range(ranks) if d & ~done == 0
        ]
        got = lax.ppermute(pivot, PLANE, pairs)
        pivot = jnp.where((row & ~done) == 0, pivot, got)
        done |= bit
    steps = KP // TILE
    state = factor_steps((unpack(pivot),), 0, steps // 2)

    half = rows // 2
    is_first = sub == 0
    even = here & 1 == 0
    packed = [pack(schur[:half]), pack(schur[half:])]
    straight = [(s * ranks + r, 2 * r + s) for s in range(2) for r in range(ranks)]
    crossed = [(s * ranks + r, 2 * r + 1 - s) for s in range(2) for r in range(ranks)]
    swap = [(i, i ^ 1) for i in range(2 * ranks)]
    got = lax.ppermute(jnp.where(is_first, packed[0], packed[1]), PLANE, straight)
    other = lax.ppermute(jnp.where(is_first, packed[1], packed[0]), PLANE, crossed)
    children = []
    for mine in (jnp.where(even, got, other), jnp.where(even, other, got)):
        theirs = lax.ppermute(mine, PLANE, swap)
        low, top = jnp.where(even, mine, theirs), jnp.where(even, theirs, mine)
        children.append(jnp.concatenate([unpack(low), unpack(top)], axis=0))
    places = jnp.concatenate(
        [
            place((here >> 1) * child_rows, child_rows, here * group_rows + jnp.arange(group_rows)),
            place(col * child_cols, child_cols, col * group_cols + jnp.arange(group_cols)),
        ],
        axis=1,
    )
    current = assemble(places, block_pattern, parent_front, *children)

    first_col = col == 0
    lead = unpack(tree_spread(pack(current[:, :KP])))
    lead = jnp.where(first_col, current[:, :KP], lead)
    raw_rows = pack(current[:KP])
    raw_packed = plane_spread(raw_rows[:KP], here)
    raw_power = plane_spread(raw_rows[KP:], here)
    raw = unpack(jnp.concatenate([raw_packed, raw_power], axis=0))
    _, lower, inverse = factor_steps(state, steps // 2, steps)
    global_rows = here * local_rows + jnp.arange(local_rows, dtype=jnp.int32)
    global_cols = col * local_cols + jnp.arange(local_cols, dtype=jnp.int32)
    below = jnp.where((global_rows >= KP)[:, None], nt(lead, inverse, high), 0.0)
    current = current - nn(below, nn(inverse, raw, high), high)
    edge = jnp.concatenate([lower, jnp.zeros((local_rows - KP, KP), jnp.float32)], axis=0)
    edge = jnp.where((global_rows < KP)[:, None], edge, below)
    merged = jnp.where(first_col, edge, current[:, :KP])
    current = lax.dynamic_update_slice(current, merged, (0, 0))
    upper_mask = (global_rows[:, None] < KP) & (global_cols[None, :] > global_rows[:, None])
    return jnp.where(upper_mask, 0.0, current)


def solution(mesh):
    return jax.shard_map(
        local,
        mesh=mesh,
        in_specs=(
            P("sub", "row", "col"),
            P("sub", "row", "col"),
            P("sub", "col", None),
            P(),
            P(PLANE, "col"),
            P(PLANE, "col"),
        ),
        out_specs=P(PLANE, "col"),
        check_vma=False,
    )
```

```python
import functools

import jax
import jax.numpy as jnp
from jax import lax
from jax.experimental import pallas as pl
from jax.experimental.pallas import tpu as pltpu
from jax.sharding import PartitionSpec as P

BLK = 256
PSTEPS = 2
KP = PSTEPS * BLK
TILE = 128
PLANE = ("sub", "row")


high = lax.Precision.HIGH


def nt(a, b, precision=None):
    return lax.dot_general(
        a, b, (((1,), (1,)), ((), ())), precision=precision, preferred_element_type=jnp.float32
    )


def nn(a, b, precision=None):
    return lax.dot_general(
        a, b, (((1,), (0,)), ((), ())), precision=precision, preferred_element_type=jnp.float32
    )


def wheel(x, distance):
    n = lax.axis_size("col")
    return lax.ppermute(x, "col", [(i, (i + distance) % n) for i in range(n)])


def chip_bits():
    return [1 << b for b in range(1, lax.axis_size("row").bit_length() - 1)]


def row_pass(x, owner, cols, bits, done):
    rows, n = lax.axis_size("row"), lax.axis_size("col")
    away = lax.axis_index("row") ^ owner(lax.axis_index("col"))
    for bit in bits:
        pairs = []
        for c in cols:
            for d in range(rows):
                if d & ~done == 0:
                    pairs.append(((owner(c) ^ d) * n + c, (owner(c) ^ d ^ bit) * n + c))
        got = lax.ppermute(x, ("row", "col"), pairs)
        x = jnp.where((away & ~done) == 0, x, got)
        done |= bit
    return x


def row_double(x, bits):
    rows = lax.axis_size("row")
    for bit in bits:
        got = lax.ppermute(x, "row", [(i, i ^ bit) for i in range(rows)])
        x = jnp.concatenate([x, got], axis=-2)
    return x


def line_blocks(units):
    n, col = lax.axis_size("col"), lax.axis_index("col")

    def side(t, up):
        if 2 * t < n:
            return units[t][0 if up else 1]
        keep = col >= t if up else col < t
        return jnp.where(keep, units[t][0], jnp.zeros_like(units[t][0]))

    out = [units[0][0]]
    for m in range(1, n):
        out.append(units[m][0] if 2 * m == n else side(m, True) + side(n - m, False))
    return out


def tree_spread(x):
    n = lax.axis_size("col")
    col = lax.axis_index("col")
    step = n // 2
    while step:
        got = lax.ppermute(x, "col", [(i, i + step) for i in range(0, n, 2 * step)])
        x = jnp.where(col & (2 * step - 1) == step, got, x)
        step //= 2
    return x


def plane_spread(x, here):
    rows, subs = lax.axis_size("row"), lax.axis_size("sub")
    across = [rows << b for b in range(subs.bit_length() - 1)]
    along = [1 << b for b in range(1, rows.bit_length() - 1)]
    half = x.shape[0] // 2
    out = []
    for part, bits in ((x[:half], along + across + [1]), (x[half:], across + along + [1])):
        done = 0
        for bit in bits:
            pairs = [(d, d ^ bit) for d in range(rows * subs) if d & ~done == 0]
            got = lax.ppermute(part, PLANE, pairs)
            part = jnp.where((here & ~done) == 0, part, got)
            done |= bit
        out.append(part)
    return jnp.concatenate(out, axis=0)


def pack(x, power=None):
    if power is None:
        top = jnp.maximum(jnp.max(jnp.abs(x)), 1e-30)
        power = jnp.ceil(jnp.log2(top))
    body = (x * jnp.exp2(-power)).astype(jnp.float16)
    return jnp.concatenate([body, jnp.full((16, x.shape[1]), power, jnp.float16)], axis=0)


def power_of(packed):
    return packed[-1, -1].astype(jnp.float32)


def unpack(packed):
    return packed[:-16].astype(jnp.float32) * jnp.exp2(power_of(packed))


def split(x):
    top = x.astype(jnp.bfloat16)
    return top, (x - top.astype(jnp.float32)).astype(jnp.bfloat16)


def product(a, b, form):
    (a0, a1), (b0, b1) = split(a), split(b)
    return form(a0, b0) + (form(a0, b1) + form(a1, b0))


def eliminate(block):
    t = block.shape[0]
    lane = lax.broadcasted_iota(jnp.int32, (8, t), 1)
    sub = lax.broadcasted_iota(jnp.int32, (8, t), 0)
    rows = [block[8 * i : 8 * i + 8] for i in range(t // 8)]
    inverse = [jnp.where(lane == sub + 8 * i, 1.0, 0.0) for i in range(t // 8)]

    def wide(x):
        return jnp.broadcast_to(x, (8, t))

    for j in range(0, t, 2):
        q, p = divmod(j, 8)
        r1, r2 = wide(rows[q][p : p + 1]), wide(rows[q][p + 1 : p + 2])
        e1, e2 = wide(inverse[q][p : p + 1]), wide(inverse[q][p + 1 : p + 2])
        a, b, c = wide(r1[:, j : j + 1]), wide(r1[:, j + 1 : j + 2]), wide(r2[:, j + 1 : j + 2])
        over = 1.0 / a
        ratio = b * over
        under = 1.0 / (c - b * ratio)
        r2, e2 = r2 - ratio * r1, e2 - ratio * e1
        r1, e1, r2, e2 = r1 * over, e1 * over, r2 * under, e2 * under
        for i in range(q, t // 8):
            f1 = wide(rows[i][:, j : j + 1])
            f2 = wide(rows[i][:, j + 1 : j + 2]) - f1 * ratio
            if i == q:
                f1 = jnp.where(sub > p, f1, 0.0)
                f2 = jnp.where(sub > p + 1, f2, 0.0)
            rows[i] = rows[i] - f1 * r1 - f2 * r2
            inverse[i] = inverse[i] - f1 * e1 - f2 * e2
    return jnp.concatenate(rows, 0), jnp.concatenate(inverse, 0)


def factor_kernel(first, last, *refs):
    work_ref, lower_ref, inverse_ref = refs[-3:]
    size = work_ref.shape[0]
    if first == 0:
        work_ref[...] = refs[0][...]
        lower_ref[...] = jnp.zeros_like(lower_ref)
        inverse_ref[...] = jnp.zeros_like(inverse_ref)
    else:
        for source, target in zip(refs[:3], refs[3:]):
            target[...] = source[...]
    r = lax.broadcasted_iota(jnp.int32, (TILE, TILE), 0)
    c = lax.broadcasted_iota(jnp.int32, (TILE, TILE), 1)

    def step(b, carry):
        at = pl.multiple_of(b * TILE, TILE)
        here = pl.ds(at, TILE)
        upper, unit = eliminate(work_ref[here, here])
        pivots = jnp.sum(jnp.where(r == c, upper, 0.0), axis=1, keepdims=True)
        root = 1.0 / jnp.sqrt(pivots)
        diagonal = jnp.where(c >= r, upper * root, 0.0).T
        local = unit * root
        column = product(work_ref[:, here], local, nt)
        ids = lax.broadcasted_iota(jnp.int32, (size, TILE), 0)
        column = jnp.where(ids >= at + TILE, column, 0.0)
        work_ref[...] = work_ref[...] - product(column, column, nt)
        known = product(lower_ref[here, :], inverse_ref[...], nn)
        rr = lax.broadcasted_iota(jnp.int32, (TILE, size), 0)
        cc = lax.broadcasted_iota(jnp.int32, (TILE, size), 1)
        inverse_ref[here, :] = product(local, jnp.where(cc == rr + at, 1.0, 0.0) - known, nn)
        lower_ref[:, here] = column
        lower_ref[here, here] = diagonal
        return carry

    lax.fori_loop(first, last, step, 0)


def factor_steps(state, first, last):
    shape = jax.ShapeDtypeStruct(state[0].shape, jnp.float32)
    return pl.pallas_call(
        functools.partial(factor_kernel, first, last),
        out_shape=[shape] * 3,
        cost_estimate=pl.CostEstimate(
            flops=(last - first) * 10**10, transcendentals=0, bytes_accessed=3 * 2**21
        ),
        name="factor_pivot",
    )(*state)


def assemble_kernel(where_ref, pattern_ref, parent_ref, *refs):
    out_ref = refs[-1]
    i = pl.program_id(0)
    group_cols = parent_ref.shape[1] // BLK
    group_rows = pl.num_programs(0)
    for k in range(group_cols):
        cols = slice(k * BLK, (k + 1) * BLK)
        value = parent_ref[:, cols] * pattern_ref[i, k].astype(jnp.float32)
        for s, ref in enumerate(refs[:-1]):
            source = where_ref[s, group_rows + k]
            hit = jnp.logical_and(where_ref[s, i] >= 0, source >= 0)
            block = ref[:, pl.ds(pl.multiple_of(jnp.maximum(source, 0) * BLK, BLK), BLK)]
            value = value + jnp.where(hit, block, 0.0)
        out_ref[:, cols] = value


def assemble(places, pattern, parent, *children):
    rows, cols = parent.shape

    def source(s):
        shape = (BLK, children[s].shape[1])
        return pl.BlockSpec(shape, lambda i, w, p: (jnp.maximum(w[s, i], 0), 0))

    return pl.pallas_call(
        assemble_kernel,
        out_shape=jax.ShapeDtypeStruct(parent.shape, jnp.float32),
        grid_spec=pltpu.PrefetchScalarGridSpec(
            num_scalar_prefetch=2,
            grid=(rows // BLK,),
            in_specs=[pl.BlockSpec((BLK, cols), lambda i, w, p: (i, 0))]
            + [source(s) for s in range(len(children))],
            out_specs=pl.BlockSpec((BLK, cols), lambda i, w, p: (i, 0)),
        ),
        name="assemble",
    )(places, pattern, parent, *children)


def local(child_update, child_coupling, pivot_inverse, child_map, parent_front, block_pattern):
    update, coupling, inverse_rows = child_update[0], child_coupling[0], pivot_inverse[0]
    rows, width = update.shape
    depth = coupling.shape[1]
    full_depth = inverse_rows.shape[1]
    n, ranks = lax.axis_size("col"), lax.axis_size("row")
    col, row, sub = lax.axis_index("col"), lax.axis_index("row"), lax.axis_index("sub")
    here = sub * ranks + row
    local_rows, local_cols = parent_front.shape

    shift = (rows // width).bit_length() - 1
    owner = lambda c: c >> shift
    share = inverse_rows.shape[0] // ranks
    group_rows, group_cols = local_rows // BLK, local_cols // BLK
    child_rows, child_cols = rows // BLK, width // BLK
    home = (n - 1) // 2

    def place(first, count, targets):
        inside = lax.dynamic_slice_in_dim(child_map, first, count, 1)
        match = inside[:, None, :] == targets[None, :, None]
        return jnp.where(match.any(-1), jnp.argmax(match, axis=-1), -1).astype(jnp.int32)

    def slot(m):
        return jnp.where(col >= m, col - m, col - m + n)

    def in_order(blocks, axis):
        size = blocks[0].shape[axis]
        shape = tuple(d * (n if a == axis else 1) for a, d in enumerate(blocks[0].shape))
        out = jnp.zeros(shape, blocks[0].dtype)
        for m, block in enumerate(blocks):
            out = lax.dynamic_update_slice_in_dim(out, block, slot(m) * size, axis)
        return out

    pivots = jnp.arange(PSTEPS)
    pivot_places = lax.dynamic_slice_in_dim(
        jnp.concatenate([place(0, child_rows, pivots), place(0, child_cols, pivots)], axis=1),
        sub, 1, 0,
    )
    base = jnp.where(here == 0, parent_front[:KP, :KP], 0.0)
    ones = jnp.where(here == 0, block_pattern[:PSTEPS, :PSTEPS], 1)
    pivot_update = assemble(pivot_places, ones, base, update)
    pivot_coupling = []
    for i in range(PSTEPS):
        at = pivot_places[0, i]
        block = lax.dynamic_slice_in_dim(coupling, jnp.maximum(at, 0) * BLK, BLK, 0)
        pivot_coupling.append(jnp.where(at >= 0, block, jnp.zeros_like(block)))
    pivot_coupling = jnp.concatenate(pivot_coupling, axis=0)
    pivot_parts = [
        pivot_coupling
        if k == home
        else lax.ppermute(pivot_coupling, ("row", "col"), [(k, home)])
        for k in range(n)
    ]
    if home:
        pivot_update = lax.ppermute(pivot_update, ("row", "col"), [(0, home)])

    def slab(x):
        if width == rows:
            return x
        return lax.dynamic_slice_in_dim(x, col * width - (owner(col) << shift) * width, width, 0)

    mine = lax.dynamic_slice_in_dim(inverse_rows, row * share, share, 0)
    chips = chip_bits()
    columns = {0: (list(range(n)),)}
    for t in range(1, n):
        right, left = list(range(t, n)), list(range(n - t))
        columns[t] = (right, left) if 2 * t < n else (right + left,)
    units, passed, spread = {0: (coupling,)}, {}, {}

    def along(t):
        return [row_pass(slab(u), owner, c, chips, 0) for u, c in zip(units[t], columns[t])]

    def across(t):
        return [row_pass(u, owner, c, [1], sum(chips)) for u, c in zip(passed[t], columns[t])]

    ups = downs = coupling
    far = far_inverse = None
    for t in range(1, n):
        ups = lax.ppermute(ups, "col", [(i, i + 1) for i in range(t - 1, n - 1)])
        downs = lax.ppermute(downs, "col", [(i + 1, i) for i in range(n - t)])
        now = {"line": [ups, downs], "along": along(t - 1)}
        if t > 1:
            now["across"] = across(t - 2)
        if t == 1:
            now["far"] = [wheel(mine, d) for d in range(1, n)]
            now["own"] = row_double(mine, chips)
            now["lead"] = pivot_parts + [pivot_update]
        if t == 2:
            far_inverse = row_double(jnp.stack(far), chips)
            own_inverse = row_double(own_inverse, [1])
            now["own"] = own_inverse
        if t == n - 1:
            now["far"] = far_inverse
        now = lax.optimization_barrier(now)
        ups, downs = now["line"]
        units[t] = (ups, downs) if 2 * t < n else (ups + downs,)
        passed[t - 1] = now["along"]
        if t > 1:
            spread[t - 2] = now["across"]
        if t == 1:
            far, own_inverse = now["far"], now["own"]
            pivot_parts, pivot_update = now["lead"][:-1], now["lead"][-1]
        if t == 2:
            own_inverse = now["own"]
        if t == n - 1:
            far_inverse = now["far"]
    far_inverse = row_double(far_inverse, [1])
    inverse_factor = in_order([own_inverse] + [far_inverse[i] for i in range(n - 1)], 0)
    deep = inverse_rows.shape[0]

    def panel_of(x):
        parts = []
        for j in range(n):
            upto = (j + 1) * deep
            parts.append(nt(x[:, :upto], inverse_factor[j * deep : upto, :upto]))
        return jnp.concatenate([p.astype(jnp.bfloat16) for p in parts], axis=1)

    pivot_panel = panel_of(jnp.concatenate(pivot_parts, axis=1))
    sent = pack(pivot_update - nt(pivot_panel, pivot_panel))
    last, sent, spread[n - 2] = lax.optimization_barrier((along(n - 1), sent, across(n - 2)))
    passed[n - 1] = last
    pivot = jnp.where(col == home, sent, jnp.zeros_like(sent))
    for k in range(n):
        if k != home:
            pivot = pivot + lax.ppermute(sent, ("row", "col"), [(home, k)])
    spread[n - 1] = across(n - 1)
    row_panel = panel_of(in_order(line_blocks(units), 1))
    pivot, row_panel, last = lax.optimization_barrier((pivot, row_panel, spread[n - 1]))
    spread[n - 1] = last
    got = lax.ppermute(pivot, PLANE, [(0, ranks), (ranks, 0)])
    col_panel = panel_of(in_order(line_blocks(spread), 1))
    got, col_panel = lax.optimization_barrier((got, col_panel))
    power = jnp.maximum(power_of(pivot), power_of(got)) + 1
    pivot = pack(unpack(pivot) + unpack(got), power)

    def onward(pivot, bits, done):
        for bit in bits:
            pairs = [
                (s * ranks + d, s * ranks + (d ^ bit))
                for s in range(2) for d in range(ranks) if d & ~done == 0
            ]
            got = lax.ppermute(pivot, PLANE, pairs)
            pivot = jnp.where((row & ~done) == 0, pivot, got)
            done |= bit
        return pivot

    pivot = onward(pivot, chips, 0)
    schur = update - nt(row_panel, col_panel)
    pivot, schur = lax.optimization_barrier((pivot, schur))
    pivot = onward(pivot, [1], sum(chips))
    steps = KP // TILE
    state = factor_steps((unpack(pivot),), 0, steps // 2)

    half = rows // 2
    is_first = sub == 0
    even = here & 1 == 0
    packed = [pack(schur[:half]), pack(schur[half:])]
    straight = [(s * ranks + r, 2 * r + s) for s in range(2) for r in range(ranks)]
    crossed = [(s * ranks + r, 2 * r + 1 - s) for s in range(2) for r in range(ranks)]
    swap = [(i, i ^ 1) for i in range(2 * ranks)]
    got = lax.ppermute(jnp.where(is_first, packed[0], packed[1]), PLANE, straight)
    other = lax.ppermute(jnp.where(is_first, packed[1], packed[0]), PLANE, crossed)
    got, other, state = lax.optimization_barrier((got, other, state))
    children = []
    for mine in (jnp.where(even, got, other), jnp.where(even, other, got)):
        theirs = lax.ppermute(mine, PLANE, swap)
        low, top = jnp.where(even, mine, theirs), jnp.where(even, theirs, mine)
        children.append(jnp.concatenate([unpack(low), unpack(top)], axis=0))
    places = jnp.concatenate(
        [
            place((here >> 1) * child_rows, child_rows, here * group_rows + jnp.arange(group_rows)),
            place(col * child_cols, child_cols, col * group_cols + jnp.arange(group_cols)),
        ],
        axis=1,
    )
    current = assemble(places, block_pattern, parent_front, *children)

    first_col = col == 0
    lead = unpack(tree_spread(pack(current[:, :KP])))
    lead = jnp.where(first_col, current[:, :KP], lead)
    raw_rows = pack(current[:KP])
    raw_packed = plane_spread(raw_rows[:KP], here)
    raw_power = plane_spread(raw_rows[KP:], here)
    raw = unpack(jnp.concatenate([raw_packed, raw_power], axis=0))
    _, lower, inverse = factor_steps(state, steps // 2, steps)
    global_rows = here * local_rows + jnp.arange(local_rows, dtype=jnp.int32)
    global_cols = col * local_cols + jnp.arange(local_cols, dtype=jnp.int32)
    below = jnp.where((global_rows >= KP)[:, None], nt(lead, inverse, high), 0.0)
    current = current - nn(below, nn(inverse, raw, high), high)
    edge = jnp.concatenate([lower, jnp.zeros((local_rows - KP, KP), jnp.float32)], axis=0)
    edge = jnp.where((global_rows < KP)[:, None], edge, below)
    merged = jnp.where(first_col, edge, current[:, :KP])
    current = lax.dynamic_update_slice(current, merged, (0, 0))
    upper_mask = (global_rows[:, None] < KP) & (global_cols[None, :] > global_rows[:, None])
    return jnp.where(upper_mask, 0.0, current)


def solution(mesh):
    return jax.shard_map(
        local,
        mesh=mesh,
        in_specs=(
            P("sub", "row", "col"),
            P("sub", "row", "col"),
            P("sub", "col", None),
            P(),
            P(PLANE, "col"),
            P(PLANE, "col"),
        ),
        out_specs=P(PLANE, "col"),
        check_vma=False,
    )
```

```python
import functools

import jax
import jax.numpy as jnp
from jax import lax
from jax.experimental import pallas as pl
from jax.experimental.pallas import tpu as pltpu
from jax.sharding import PartitionSpec as P

BLK = 256
PSTEPS = 2
KP = PSTEPS * BLK
TILE = 128
HEADROOM = 14.0
PLANE = ("sub", "row")


high = lax.Precision.HIGH


def nt(a, b, precision=None):
    return lax.dot_general(
        a, b, (((1,), (1,)), ((), ())), precision=precision, preferred_element_type=jnp.float32
    )


def nn(a, b, precision=None):
    return lax.dot_general(
        a, b, (((1,), (0,)), ((), ())), precision=precision, preferred_element_type=jnp.float32
    )


def chip_bits():
    return [1 << b for b in range(1, lax.axis_size("row").bit_length() - 1)]


def row_pass(x, owner, cols, bits, done):
    rows, n = lax.axis_size("row"), lax.axis_size("col")
    away = lax.axis_index("row") ^ owner(lax.axis_index("col"))
    for bit in bits:
        pairs = []
        for c in cols:
            for d in range(rows):
                if d & ~done == 0:
                    pairs.append(((owner(c) ^ d) * n + c, (owner(c) ^ d ^ bit) * n + c))
        got = lax.ppermute(x, ("row", "col"), pairs)
        x = jnp.where((away & ~done) == 0, x, got)
        done |= bit
    return x


def line_blocks(units):
    n, col = lax.axis_size("col"), lax.axis_index("col")

    def side(t, up):
        if 2 * t < n:
            return units[t][0 if up else 1]
        keep = col >= t if up else col < t
        return jnp.where(keep, units[t][0], jnp.zeros_like(units[t][0]))

    out = [units[0][0]]
    for m in range(1, n):
        out.append(units[m][0] if 2 * m == n else side(m, True) + side(n - m, False))
    return out


def tree_stages(x):
    n = lax.axis_size("col")
    col = lax.axis_index("col")
    step = n // 2
    while step:
        got = lax.ppermute(x, "col", [(i, i + step) for i in range(0, n, 2 * step)])
        x = jnp.where(col & (2 * step - 1) == step, got, x)
        step //= 2
        yield x


def plane_stages(pieces, here):
    rows, subs = lax.axis_size("row"), lax.axis_size("sub")
    across = [rows << b for b in range(subs.bit_length() - 1)]
    along = chip_bits()
    orders = (along + across + [1], across + along + [1])
    done = [0, 0]
    for bits in zip(*orders):
        out = []
        for k, bit in enumerate(bits):
            pairs = [(d, d ^ bit) for d in range(rows * subs) if d & ~done[k] == 0]
            got = lax.ppermute(pieces[k], PLANE, pairs)
            out.append(jnp.where((here & ~done[k]) == 0, pieces[k], got))
            done[k] |= bit
        pieces = out
        yield pieces


def pack(x, power=None):
    if power is None:
        power = exponent(jnp.max(jnp.abs(x)))
    body = (x * jnp.exp2(HEADROOM - power)).astype(jnp.float16)
    return jnp.concatenate([body, jnp.full((16, x.shape[1]), power, jnp.float16)], axis=0)


def exponent(bound):
    return jnp.ceil(jnp.log2(jnp.maximum(bound, 1e-30)))


def powers(packed):
    return packed[-16:-15].astype(jnp.float32)


def unpack(packed):
    return packed[:-16].astype(jnp.float32) * jnp.exp2(powers(packed) - HEADROOM)


def split(x):
    top = x.astype(jnp.bfloat16)
    return top, (x - top.astype(jnp.float32)).astype(jnp.bfloat16)


def product(a, b, form):
    (a0, a1), (b0, b1) = split(a), split(b)
    return form(a0, b0) + (form(a0, b1) + form(a1, b0))


def eliminate(block):
    t = block.shape[0]
    lane = lax.broadcasted_iota(jnp.int32, (8, t), 1)
    sub = lax.broadcasted_iota(jnp.int32, (8, t), 0)
    rows = [block[8 * i : 8 * i + 8] for i in range(t // 8)]
    inverse = [jnp.where(lane == sub + 8 * i, 1.0, 0.0) for i in range(t // 8)]

    def wide(x):
        return jnp.broadcast_to(x, (8, t))

    for j in range(0, t, 2):
        q, p = divmod(j, 8)
        r1, r2 = wide(rows[q][p : p + 1]), wide(rows[q][p + 1 : p + 2])
        e1, e2 = wide(inverse[q][p : p + 1]), wide(inverse[q][p + 1 : p + 2])
        a, b, c = wide(r1[:, j : j + 1]), wide(r1[:, j + 1 : j + 2]), wide(r2[:, j + 1 : j + 2])
        over = 1.0 / a
        ratio = b * over
        under = 1.0 / (c - b * ratio)
        r2, e2 = r2 - ratio * r1, e2 - ratio * e1
        r1, e1, r2, e2 = r1 * over, e1 * over, r2 * under, e2 * under
        for i in range(q, t // 8):
            f1 = wide(rows[i][:, j : j + 1])
            f2 = wide(rows[i][:, j + 1 : j + 2]) - f1 * ratio
            if i == q:
                f1 = jnp.where(sub > p, f1, 0.0)
                f2 = jnp.where(sub > p + 1, f2, 0.0)
            rows[i] = rows[i] - f1 * r1 - f2 * r2
            inverse[i] = inverse[i] - f1 * e1 - f2 * e2
    return jnp.concatenate(rows, 0), jnp.concatenate(inverse, 0)


def factor_kernel(first, last, *refs):
    work_ref, lower_ref, inverse_ref = refs[-3:]
    size = work_ref.shape[0]
    if first == 0:
        work_ref[...] = refs[0][...]
        lower_ref[...] = jnp.zeros_like(lower_ref)
        inverse_ref[...] = jnp.zeros_like(inverse_ref)
    else:
        for source, target in zip(refs[:3], refs[3:]):
            target[...] = source[...]
    r = lax.broadcasted_iota(jnp.int32, (TILE, TILE), 0)
    c = lax.broadcasted_iota(jnp.int32, (TILE, TILE), 1)

    def step(b, carry):
        at = pl.multiple_of(b * TILE, TILE)
        here = pl.ds(at, TILE)
        upper, unit = eliminate(work_ref[here, here])
        pivots = jnp.sum(jnp.where(r == c, upper, 0.0), axis=1, keepdims=True)
        root = 1.0 / jnp.sqrt(pivots)
        diagonal = jnp.where(c >= r, upper * root, 0.0).T
        local = unit * root
        column = product(work_ref[:, here], local, nt)
        ids = lax.broadcasted_iota(jnp.int32, (size, TILE), 0)
        column = jnp.where(ids >= at + TILE, column, 0.0)
        work_ref[...] = work_ref[...] - product(column, column, nt)
        known = product(lower_ref[here, :], inverse_ref[...], nn)
        rr = lax.broadcasted_iota(jnp.int32, (TILE, size), 0)
        cc = lax.broadcasted_iota(jnp.int32, (TILE, size), 1)
        inverse_ref[here, :] = product(local, jnp.where(cc == rr + at, 1.0, 0.0) - known, nn)
        lower_ref[:, here] = column
        lower_ref[here, here] = diagonal
        return carry

    lax.fori_loop(first, last, step, 0)


def factor_steps(state, first, last):
    shape = jax.ShapeDtypeStruct(state[0].shape, jnp.float32)
    return pl.pallas_call(
        functools.partial(factor_kernel, first, last),
        out_shape=[shape] * 3,
        cost_estimate=pl.CostEstimate(
            flops=(last - first) * 10**10, transcendentals=0, bytes_accessed=3 * 2**21
        ),
        name="factor_pivot",
    )(*state)


def assemble_kernel(where_ref, pattern_ref, parent_ref, *refs):
    out_ref = refs[-1]
    i = pl.program_id(0)
    group_cols = parent_ref.shape[1] // BLK
    group_rows = pl.num_programs(0)
    for k in range(group_cols):
        cols = slice(k * BLK, (k + 1) * BLK)
        value = parent_ref[:, cols] * pattern_ref[i, k].astype(jnp.float32)
        for s, ref in enumerate(refs[:-1]):
            source = where_ref[s, group_rows + k]
            hit = jnp.logical_and(where_ref[s, i] >= 0, source >= 0)
            block = ref[:, pl.ds(pl.multiple_of(jnp.maximum(source, 0) * BLK, BLK), BLK)]
            value = value + jnp.where(hit, block, 0.0)
        out_ref[:, cols] = value


def assemble(places, pattern, parent, *children):
    rows, cols = parent.shape

    def source(s):
        shape = (BLK, children[s].shape[1])
        return pl.BlockSpec(shape, lambda i, w, p: (jnp.maximum(w[s, i], 0), 0))

    return pl.pallas_call(
        assemble_kernel,
        out_shape=jax.ShapeDtypeStruct(parent.shape, jnp.float32),
        grid_spec=pltpu.PrefetchScalarGridSpec(
            num_scalar_prefetch=2,
            grid=(rows // BLK,),
            in_specs=[pl.BlockSpec((BLK, cols), lambda i, w, p: (i, 0))]
            + [source(s) for s in range(len(children))],
            out_specs=pl.BlockSpec((BLK, cols), lambda i, w, p: (i, 0)),
        ),
        name="assemble",
    )(places, pattern, parent, *children)


def local(child_update, child_coupling, pivot_inverse, child_map, parent_front, block_pattern):
    update, coupling, inverse_rows = child_update[0], child_coupling[0], pivot_inverse[0]
    rows, width = update.shape
    depth = coupling.shape[1]
    full_depth = inverse_rows.shape[1]
    n, ranks = lax.axis_size("col"), lax.axis_size("row")
    col, row, sub = lax.axis_index("col"), lax.axis_index("row"), lax.axis_index("sub")
    here = sub * ranks + row
    local_rows, local_cols = parent_front.shape

    shift = (rows // width).bit_length() - 1
    owner = lambda c: c >> shift
    share = inverse_rows.shape[0] // ranks
    group_rows, group_cols = local_rows // BLK, local_cols // BLK
    child_rows, child_cols = rows // BLK, width // BLK
    home = (n - 1) // 2

    def place(first, count, targets):
        inside = lax.dynamic_slice_in_dim(child_map, first, count, 1)
        match = inside[:, None, :] == targets[None, :, None]
        return jnp.where(match.any(-1), jnp.argmax(match, axis=-1), -1).astype(jnp.int32)

    def slot(m):
        return jnp.where(col >= m, col - m, col - m + n)

    def in_order(blocks, axis):
        size = blocks[0].shape[axis]
        shape = tuple(d * (n if a == axis else 1) for a, d in enumerate(blocks[0].shape))
        out = jnp.zeros(shape, blocks[0].dtype)
        for m, block in enumerate(blocks):
            out = lax.dynamic_update_slice_in_dim(out, block, slot(m) * size, axis)
        return out

    pivots = jnp.arange(PSTEPS)
    pivot_places = lax.dynamic_slice_in_dim(
        jnp.concatenate([place(0, child_rows, pivots), place(0, child_cols, pivots)], axis=1),
        sub, 1, 0,
    )
    base = jnp.where(here == 0, parent_front[:KP, :KP], 0.0)
    ones = jnp.where(here == 0, block_pattern[:PSTEPS, :PSTEPS], 1)
    pivot_update = assemble(pivot_places, ones, base, update)
    if home:
        pivot_update = lax.ppermute(pivot_update, ("row", "col"), [(0, home)])

    def slab(x):
        if width == rows:
            return x
        return lax.dynamic_slice_in_dim(x, col * width - (owner(col) << shift) * width, width, 0)

    mine = lax.dynamic_slice_in_dim(inverse_rows, row * share, share, 0)
    inverse_factor = lax.all_gather(mine, ("col", "row"), axis=0, tiled=True)
    chips = chip_bits()
    units = {0: (coupling,)}
    ups = downs = coupling
    for t in range(1, n):
        ups = lax.ppermute(ups, "col", [(i, i + 1) for i in range(t - 1, n - 1)])
        downs = lax.ppermute(downs, "col", [(i + 1, i) for i in range(n - t)])
        now = {"line": [ups, downs]}
        if t == 2:
            now["lead"] = pivot_update
            now["top"] = jnp.max(jnp.abs(parent_front))
        now = lax.optimization_barrier(now)
        ups, downs = now["line"]
        units[t] = (ups, downs) if 2 * t < n else (ups + downs,)
        if t == 2:
            pivot_update, parent_top = now["lead"], now["top"]

    def along(x):
        return row_pass(slab(x), owner, range(n), chips, 0)

    def across(x):
        return row_pass(x, owner, range(n), [1], sum(chips))

    deep = full_depth // 2

    def panel_of(x):
        low = nt(x[:, :deep], inverse_factor[:deep, :deep]).astype(jnp.bfloat16)
        return low, nt(x, inverse_factor[deep:]).astype(jnp.bfloat16)

    def reduce_by(value, left, right):
        return value - (nt(left[0], right[0]) + nt(left[1], right[1]))

    row_panel = panel_of(in_order(line_blocks(units), 1))
    passed = [along(p) for p in row_panel]
    pivot_panel = []
    for part in row_panel:
        picked = []
        for i in range(PSTEPS):
            at = pivot_places[0, i]
            block = lax.dynamic_slice_in_dim(part, jnp.maximum(at, 0) * BLK, BLK, 0)
            picked.append(jnp.where(at >= 0, block, jnp.zeros_like(block)))
        pivot_panel.append(jnp.concatenate(picked, axis=0))
    sent = pack(reduce_by(pivot_update, pivot_panel, pivot_panel))
    pivot = jnp.where(col == home, sent, jnp.zeros_like(sent))
    for k in range(n):
        if k != home:
            pivot = pivot + lax.ppermute(sent, ("row", "col"), [(home, k)])
    pivot, passed[0] = lax.optimization_barrier((pivot, passed[0]))
    got = lax.ppermute(pivot, PLANE, [(0, ranks), (ranks, 0)])
    col_panel = [across(passed[0])]
    got, passed[1], col_panel[0] = lax.optimization_barrier((got, passed[1], col_panel[0]))
    col_panel.append(across(passed[1]))
    power = jnp.max(jnp.maximum(powers(pivot), powers(got))) + 1
    pivot = pack(unpack(pivot) + unpack(got), power)

    def onward(pivot, bits, done):
        for bit in bits:
            pairs = [
                (s * ranks + d, s * ranks + (d ^ bit))
                for s in range(2) for d in range(ranks) if d & ~done == 0
            ]
            got = lax.ppermute(pivot, PLANE, pairs)
            pivot = jnp.where((row & ~done) == 0, pivot, got)
            done |= bit
        return pivot

    pivot = onward(pivot, chips, 0)
    schur = reduce_by(update, row_panel, col_panel)
    pivot, schur = lax.optimization_barrier((pivot, schur))
    pivot = onward(pivot, [1], sum(chips))
    steps = KP // TILE
    state = factor_steps((unpack(pivot),), 0, steps // 2)

    half = rows // 2
    is_first = sub == 0
    even = here & 1 == 0
    packed = [pack(schur[:half]), pack(schur[half:])]
    straight = [(s * ranks + r, 2 * r + s) for s in range(2) for r in range(ranks)]
    crossed = [(s * ranks + r, 2 * r + 1 - s) for s in range(2) for r in range(ranks)]
    swap = [(i, i ^ 1) for i in range(2 * ranks)]
    got = lax.ppermute(jnp.where(is_first, packed[0], packed[1]), PLANE, straight)
    other = lax.ppermute(jnp.where(is_first, packed[1], packed[0]), PLANE, crossed)
    got, other, state = lax.optimization_barrier((got, other, state))
    pieces = [got, other] + [lax.ppermute(p, PLANE, swap) for p in (got, other)]
    core = here & 1
    child_of, half_of = (core, 1 - core, 1 - core, core), (core, core, 1 - core, 1 - core)
    row_places = place((here >> 1) * child_rows, child_rows, here * group_rows + jnp.arange(group_rows))
    col_places = place(col * child_cols, child_cols, col * group_cols + jnp.arange(group_cols))
    half_blocks = half // BLK
    places = []
    for s, h in zip(child_of, half_of):
        r = jnp.where(s == 0, row_places[0], row_places[1]) - h * half_blocks
        r = jnp.where((r >= 0) & (r < half_blocks), r, -1)
        places.append(jnp.concatenate([r, jnp.where(s == 0, col_places[0], col_places[1])]))
    highest = functools.reduce(jnp.maximum, [powers(p) for p in pieces])
    power = exponent(parent_top + 2 * jnp.exp2(jnp.max(highest)))
    current = assemble(jnp.stack(places), block_pattern, parent_front, *[unpack(p) for p in pieces])

    first_col = col == 0
    lead_stages = tree_stages(pack(current[:, :KP], power))
    raw_halves = [pack(current[: KP // 2], power), pack(current[KP // 2 : KP], power)]
    raw_stages = plane_stages(raw_halves, here)
    lead, raw_halves = next(lead_stages), next(raw_stages)
    state, raw_halves = lax.optimization_barrier((state, raw_halves))
    for lead in lead_stages:
        pass
    for raw_halves in raw_stages:
        pass
    lead = jnp.where(first_col, current[:, :KP], unpack(lead))
    raw = jnp.concatenate([unpack(p) for p in raw_halves], axis=0)
    _, lower, inverse = factor_steps(state, steps // 2, steps)
    global_rows = here * local_rows + jnp.arange(local_rows, dtype=jnp.int32)
    below = jnp.where((global_rows >= KP)[:, None], nt(lead, inverse, high), 0.0)
    current = current - nn(nn(below, inverse, high), raw, high)
    edge = jnp.concatenate([lower, jnp.zeros((local_rows - KP, KP), jnp.float32)], axis=0)
    edge = jnp.where((global_rows < KP)[:, None], edge, below)
    merged = jnp.where(first_col, edge, current[:, :KP])
    current = lax.dynamic_update_slice(current, merged, (0, 0))
    global_cols = col * local_cols + jnp.arange(local_cols, dtype=jnp.int32)
    upper_mask = (global_rows[:, None] < KP) & (global_cols[None, :] > global_rows[:, None])
    return jnp.where(upper_mask, 0.0, current)


def solution(mesh):
    return jax.shard_map(
        local,
        mesh=mesh,
        in_specs=(
            P("sub", "row", "col"),
            P("sub", "row", "col"),
            P("sub", "col", None),
            P(),
            P(PLANE, "col"),
            P(PLANE, "col"),
        ),
        out_specs=P(PLANE, "col"),
        check_vma=False,
    )
```

```python
import functools

import jax
import jax.numpy as jnp
from jax import lax
from jax.experimental import pallas as pl
from jax.experimental.pallas import tpu as pltpu
from jax.sharding import PartitionSpec as P

BLK = 256
PSTEPS = 2
KP = PSTEPS * BLK
TILE = 128
HEADROOM = 14.0
PLANE = ("sub", "row")


high = lax.Precision.HIGH


def nt(a, b, precision=None):
    return lax.dot_general(
        a, b, (((1,), (1,)), ((), ())), precision=precision, preferred_element_type=jnp.float32
    )


def nn(a, b, precision=None):
    return lax.dot_general(
        a, b, (((1,), (0,)), ((), ())), precision=precision, preferred_element_type=jnp.float32
    )


def chip_bits():
    return [1 << b for b in range(1, lax.axis_size("row").bit_length() - 1)]


def row_pass(x, owner, cols, bits, done):
    rows, n = lax.axis_size("row"), lax.axis_size("col")
    away = lax.axis_index("row") ^ owner(lax.axis_index("col"))
    for bit in bits:
        pairs = []
        for c in cols:
            for d in range(rows):
                if d & ~done == 0:
                    pairs.append(((owner(c) ^ d) * n + c, (owner(c) ^ d ^ bit) * n + c))
        got = lax.ppermute(x, ("row", "col"), pairs)
        x = jnp.where((away & ~done) == 0, x, got)
        done |= bit
    return x


def line_blocks(units):
    n, col = lax.axis_size("col"), lax.axis_index("col")

    def side(t, up):
        if 2 * t < n:
            return units[t][0 if up else 1]
        keep = col >= t if up else col < t
        return jnp.where(keep, units[t][0], jnp.zeros_like(units[t][0]))

    out = [units[0][0]]
    for m in range(1, n):
        out.append(units[m][0] if 2 * m == n else side(m, True) + side(n - m, False))
    return out


def tree_stages(x):
    n = lax.axis_size("col")
    col = lax.axis_index("col")
    step = n // 2
    while step:
        got = lax.ppermute(x, "col", [(i, i + step) for i in range(0, n, 2 * step)])
        x = jnp.where(col & (2 * step - 1) == step, got, x)
        step //= 2
        yield x


def plane_stages(pieces, here):
    rows, subs = lax.axis_size("row"), lax.axis_size("sub")
    across = [rows << b for b in range(subs.bit_length() - 1)]
    along = chip_bits()
    orders = (along + across + [1], across + along + [1])
    done = [0, 0]
    for bits in zip(*orders):
        out = []
        for k, bit in enumerate(bits):
            pairs = [(d, d ^ bit) for d in range(rows * subs) if d & ~done[k] == 0]
            got = lax.ppermute(pieces[k], PLANE, pairs)
            out.append(jnp.where((here & ~done[k]) == 0, pieces[k], got))
            done[k] |= bit
        pieces = out
        yield pieces


def pack(x, power=None):
    if power is None:
        power = exponent(jnp.max(jnp.abs(x)))
    body = (x * jnp.exp2(HEADROOM - power)).astype(jnp.float16)
    return jnp.concatenate([body, jnp.full((16, x.shape[1]), power, jnp.float16)], axis=0)


def exponent(bound):
    return jnp.ceil(jnp.log2(jnp.maximum(bound, 1e-30)))


def powers(packed):
    return packed[-16:-15].astype(jnp.float32)


def unpack(packed):
    return packed[:-16].astype(jnp.float32) * jnp.exp2(powers(packed) - HEADROOM)


def split(x):
    top = x.astype(jnp.bfloat16)
    return top, (x - top.astype(jnp.float32)).astype(jnp.bfloat16)


def product(a, b, form):
    (a0, a1), (b0, b1) = split(a), split(b)
    return form(a0, b0) + (form(a0, b1) + form(a1, b0))


def eliminate(block):
    t = block.shape[0]
    lane = lax.broadcasted_iota(jnp.int32, (8, t), 1)
    sub = lax.broadcasted_iota(jnp.int32, (8, t), 0)
    rows = [block[8 * i : 8 * i + 8] for i in range(t // 8)]
    inverse = [jnp.where(lane == sub + 8 * i, 1.0, 0.0) for i in range(t // 8)]

    def wide(x):
        return jnp.broadcast_to(x, (8, t))

    for j in range(0, t, 2):
        q, p = divmod(j, 8)
        r1, r2 = wide(rows[q][p : p + 1]), wide(rows[q][p + 1 : p + 2])
        e1, e2 = wide(inverse[q][p : p + 1]), wide(inverse[q][p + 1 : p + 2])
        a, b, c = wide(r1[:, j : j + 1]), wide(r1[:, j + 1 : j + 2]), wide(r2[:, j + 1 : j + 2])
        over = 1.0 / a
        ratio = b * over
        under = 1.0 / (c - b * ratio)
        r2, e2 = r2 - ratio * r1, e2 - ratio * e1
        r1, e1, r2, e2 = r1 * over, e1 * over, r2 * under, e2 * under
        for i in range(q, t // 8):
            f1 = wide(rows[i][:, j : j + 1])
            f2 = wide(rows[i][:, j + 1 : j + 2]) - f1 * ratio
            if i == q:
                f1 = jnp.where(sub > p, f1, 0.0)
                f2 = jnp.where(sub > p + 1, f2, 0.0)
            rows[i] = rows[i] - f1 * r1 - f2 * r2
            inverse[i] = inverse[i] - f1 * e1 - f2 * e2
    return jnp.concatenate(rows, 0), jnp.concatenate(inverse, 0)


def factor_kernel(first, last, *refs):
    work_ref, lower_ref, inverse_ref = refs[-3:]
    size = work_ref.shape[0]
    if first == 0:
        work_ref[...] = refs[0][...]
        lower_ref[...] = jnp.zeros_like(lower_ref)
        inverse_ref[...] = jnp.zeros_like(inverse_ref)
    else:
        for source, target in zip(refs[:3], refs[3:]):
            target[...] = source[...]
    r = lax.broadcasted_iota(jnp.int32, (TILE, TILE), 0)
    c = lax.broadcasted_iota(jnp.int32, (TILE, TILE), 1)

    def step(b, carry):
        at = pl.multiple_of(b * TILE, TILE)
        here = pl.ds(at, TILE)
        upper, unit = eliminate(work_ref[here, here])
        pivots = jnp.sum(jnp.where(r == c, upper, 0.0), axis=1, keepdims=True)
        root = 1.0 / jnp.sqrt(pivots)
        diagonal = jnp.where(c >= r, upper * root, 0.0).T
        local = unit * root
        column = product(work_ref[:, here], local, nt)
        ids = lax.broadcasted_iota(jnp.int32, (size, TILE), 0)
        column = jnp.where(ids >= at + TILE, column, 0.0)
        work_ref[...] = work_ref[...] - product(column, column, nt)
        known = product(lower_ref[here, :], inverse_ref[...], nn)
        rr = lax.broadcasted_iota(jnp.int32, (TILE, size), 0)
        cc = lax.broadcasted_iota(jnp.int32, (TILE, size), 1)
        inverse_ref[here, :] = product(local, jnp.where(cc == rr + at, 1.0, 0.0) - known, nn)
        lower_ref[:, here] = column
        lower_ref[here, here] = diagonal
        return carry

    lax.fori_loop(first, last, step, 0)


def factor_steps(state, first, last):
    shape = jax.ShapeDtypeStruct(state[0].shape, jnp.float32)
    return pl.pallas_call(
        functools.partial(factor_kernel, first, last),
        out_shape=[shape] * 3,
        cost_estimate=pl.CostEstimate(
            flops=(last - first) * 10**10, transcendentals=0, bytes_accessed=3 * 2**21
        ),
        name="factor_pivot",
    )(*state)


def assemble_kernel(where_ref, pattern_ref, parent_ref, *refs):
    out_ref = refs[-1]
    i = pl.program_id(0)
    group_cols = parent_ref.shape[1] // BLK
    group_rows = pl.num_programs(0)
    for k in range(group_cols):
        cols = slice(k * BLK, (k + 1) * BLK)
        value = parent_ref[:, cols] * pattern_ref[i, k].astype(jnp.float32)
        for s, ref in enumerate(refs[:-1]):
            source = where_ref[s, group_rows + k]
            hit = jnp.logical_and(where_ref[s, i] >= 0, source >= 0)
            block = ref[:, pl.ds(pl.multiple_of(jnp.maximum(source, 0) * BLK, BLK), BLK)]
            value = value + jnp.where(hit, block, 0.0)
        out_ref[:, cols] = value


def assemble(places, pattern, parent, *children):
    rows, cols = parent.shape

    def source(s):
        shape = (BLK, children[s].shape[1])
        return pl.BlockSpec(shape, lambda i, w, p: (jnp.maximum(w[s, i], 0), 0))

    return pl.pallas_call(
        assemble_kernel,
        out_shape=jax.ShapeDtypeStruct(parent.shape, jnp.float32),
        grid_spec=pltpu.PrefetchScalarGridSpec(
            num_scalar_prefetch=2,
            grid=(rows // BLK,),
            in_specs=[pl.BlockSpec((BLK, cols), lambda i, w, p: (i, 0))]
            + [source(s) for s in range(len(children))],
            out_specs=pl.BlockSpec((BLK, cols), lambda i, w, p: (i, 0)),
        ),
        name="assemble",
    )(places, pattern, parent, *children)


def local(child_update, child_coupling, pivot_inverse, child_map, parent_front, block_pattern):
    update, coupling, inverse_rows = child_update[0], child_coupling[0], pivot_inverse[0]
    rows, width = update.shape
    full_depth = inverse_rows.shape[1]
    n, ranks = lax.axis_size("col"), lax.axis_size("row")
    col, row, sub = lax.axis_index("col"), lax.axis_index("row"), lax.axis_index("sub")
    here = sub * ranks + row
    local_rows, local_cols = parent_front.shape

    shift = (rows // width).bit_length() - 1
    owner = lambda c: c >> shift
    share = inverse_rows.shape[0] // ranks
    group_rows, group_cols = local_rows // BLK, local_cols // BLK
    child_rows, child_cols = rows // BLK, width // BLK
    home = (n - 1) // 2

    def place(first, count, targets):
        inside = lax.dynamic_slice_in_dim(child_map, first, count, 1)
        match = inside[:, None, :] == targets[None, :, None]
        return jnp.where(match.any(-1), jnp.argmax(match, axis=-1), -1).astype(jnp.int32)

    def slot(m):
        return jnp.where(col >= m, col - m, col - m + n)

    def in_order(blocks, axis):
        size = blocks[0].shape[axis]
        shape = tuple(d * (n if a == axis else 1) for a, d in enumerate(blocks[0].shape))
        out = jnp.zeros(shape, blocks[0].dtype)
        for m, block in enumerate(blocks):
            out = lax.dynamic_update_slice_in_dim(out, block, slot(m) * size, axis)
        return out

    pivots = jnp.arange(PSTEPS)
    pivot_places = lax.dynamic_slice_in_dim(
        jnp.concatenate([place(0, child_rows, pivots), place(0, child_cols, pivots)], axis=1),
        sub, 1, 0,
    )
    base = jnp.where(here == 0, parent_front[:KP, :KP], 0.0)
    ones = jnp.where(here == 0, block_pattern[:PSTEPS, :PSTEPS], 1)
    pivot_update = assemble(pivot_places, ones, base, update)
    if home:
        pivot_update = lax.ppermute(pivot_update, ("row", "col"), [(0, home)])

    def slab(x):
        if width == rows:
            return x
        return lax.dynamic_slice_in_dim(x, col * width - (owner(col) << shift) * width, width, 0)

    mine = lax.dynamic_slice_in_dim(inverse_rows, row * share, share, 0)
    middle, part = full_depth // 2, share // 2
    given = lax.ppermute(mine[part:, middle:], "col", [(n - 1 - c, c) for c in range(n // 2)])
    right = jnp.where(col < n // 2, given, mine[:part, middle:])
    gathered = lax.all_gather(
        jnp.concatenate([mine[:, :middle], right], axis=0), ("col", "row"), axis=0, tiled=True
    ).reshape(n, ranks, share + part, middle)
    lefts = gathered[:, :, :share].reshape(full_depth, middle)
    halves = (gathered[n // 2 :, :, share:], gathered[: n // 2, :, share:][::-1])
    rights = jnp.concatenate(halves, axis=2).reshape(full_depth - middle, middle)
    inverse_low = lefts[:middle]
    inverse_high = jnp.concatenate([lefts[middle:], rights], axis=1)
    chips = chip_bits()
    units = {0: (coupling,)}
    ups = downs = coupling
    for t in range(1, n):
        ups = lax.ppermute(ups, "col", [(i, i + 1) for i in range(t - 1, n - 1)])
        downs = lax.ppermute(downs, "col", [(i + 1, i) for i in range(n - t)])
        now = {"line": [ups, downs]}
        if t == 2:
            now["lead"] = pivot_update
            now["top"] = jnp.max(jnp.abs(parent_front))
        if t == n - 1:
            now["inverse"] = (inverse_low, inverse_high)
        now = lax.optimization_barrier(now)
        if t == n - 1:
            inverse_low, inverse_high = now["inverse"]
        ups, downs = now["line"]
        units[t] = (ups, downs) if 2 * t < n else (ups + downs,)
        if t == 2:
            pivot_update, parent_top = now["lead"], now["top"]

    def along(x):
        return row_pass(slab(x), owner, range(n), chips, 0)

    def across(x):
        return row_pass(x, owner, range(n), [1], sum(chips))

    def panel_of(x):
        low = nt(x[:, :middle], inverse_low).astype(jnp.bfloat16)
        return low, nt(x, inverse_high).astype(jnp.bfloat16)

    def reduce_by(value, left, right):
        return value - (nt(left[0], right[0]) + nt(left[1], right[1]))

    row_panel = panel_of(in_order(line_blocks(units), 1))
    passed = [along(p) for p in row_panel]
    pivot_panel = []
    for part in row_panel:
        picked = []
        for i in range(PSTEPS):
            at = pivot_places[0, i]
            block = lax.dynamic_slice_in_dim(part, jnp.maximum(at, 0) * BLK, BLK, 0)
            picked.append(jnp.where(at >= 0, block, jnp.zeros_like(block)))
        pivot_panel.append(jnp.concatenate(picked, axis=0))
    sent = pack(reduce_by(pivot_update, pivot_panel, pivot_panel))
    pivot = jnp.where(col == home, sent, jnp.zeros_like(sent))
    for k in range(n):
        if k != home:
            pivot = pivot + lax.ppermute(sent, ("row", "col"), [(home, k)])
    pivot, passed[0] = lax.optimization_barrier((pivot, passed[0]))
    got = lax.ppermute(pivot, PLANE, [(0, ranks), (ranks, 0)])
    col_panel = [across(passed[0])]
    got, passed[1], col_panel[0] = lax.optimization_barrier((got, passed[1], col_panel[0]))
    col_panel.append(across(passed[1]))
    power = jnp.max(jnp.maximum(powers(pivot), powers(got))) + 1
    pivot = pack(unpack(pivot) + unpack(got), power)

    def onward(pivot, bits, done):
        for bit in bits:
            pairs = [
                (s * ranks + d, s * ranks + (d ^ bit))
                for s in range(2) for d in range(ranks) if d & ~done == 0
            ]
            got = lax.ppermute(pivot, PLANE, pairs)
            pivot = jnp.where((row & ~done) == 0, pivot, got)
            done |= bit
        return pivot

    pivot = onward(pivot, chips, 0)
    schur = reduce_by(update, row_panel, col_panel)
    pivot, schur = lax.optimization_barrier((pivot, schur))
    pivot = onward(pivot, [1], sum(chips))
    steps = KP // TILE
    state = factor_steps((unpack(pivot),), 0, steps // 2)

    half = rows // 2
    is_first = sub == 0
    packed = [pack(schur[:half]), pack(schur[half:])]
    straight = [(s * ranks + r, 2 * r + s) for s in range(2) for r in range(ranks)]
    crossed = [(s * ranks + r, 2 * r + 1 - s) for s in range(2) for r in range(ranks)]
    swap = [(i, i ^ 1) for i in range(2 * ranks)]
    got = lax.ppermute(jnp.where(is_first, packed[0], packed[1]), PLANE, straight)
    other = lax.ppermute(jnp.where(is_first, packed[1], packed[0]), PLANE, crossed)
    got, other, state = lax.optimization_barrier((got, other, state))
    pieces = [got, other] + [lax.ppermute(p, PLANE, swap) for p in (got, other)]
    core = here & 1
    child_of, half_of = (core, 1 - core, 1 - core, core), (core, core, 1 - core, 1 - core)
    row_places = place((here >> 1) * child_rows, child_rows, here * group_rows + jnp.arange(group_rows))
    col_places = place(col * child_cols, child_cols, col * group_cols + jnp.arange(group_cols))
    half_blocks = half // BLK
    places = []
    for s, h in zip(child_of, half_of):
        r = jnp.where(s == 0, row_places[0], row_places[1]) - h * half_blocks
        r = jnp.where((r >= 0) & (r < half_blocks), r, -1)
        places.append(jnp.concatenate([r, jnp.where(s == 0, col_places[0], col_places[1])]))
    highest = functools.reduce(jnp.maximum, [powers(p) for p in pieces])
    power = exponent(parent_top + 2 * jnp.exp2(jnp.max(highest)))
    current = assemble(jnp.stack(places), block_pattern, parent_front, *[unpack(p) for p in pieces])

    first_col = col == 0
    lead_stages = tree_stages(pack(current[:, :KP], power))
    raw_halves = [pack(current[: KP // 2], power), pack(current[KP // 2 : KP], power)]
    raw_stages = plane_stages(raw_halves, here)
    lead, raw_halves = next(lead_stages), next(raw_stages)
    state, raw_halves = lax.optimization_barrier((state, raw_halves))
    for lead in lead_stages:
        pass
    for raw_halves in raw_stages:
        pass
    lead = jnp.where(first_col, current[:, :KP], unpack(lead))
    raw = jnp.concatenate([unpack(p) for p in raw_halves], axis=0)
    _, lower, inverse = factor_steps(state, steps // 2, steps)
    global_rows = here * local_rows + jnp.arange(local_rows, dtype=jnp.int32)
    below = jnp.where((global_rows >= KP)[:, None], nt(lead, inverse, high), 0.0)
    current = current - nn(nn(below, inverse, high), raw, high)
    edge = jnp.concatenate([lower, jnp.zeros((local_rows - KP, KP), jnp.float32)], axis=0)
    edge = jnp.where((global_rows < KP)[:, None], edge, below)
    merged = jnp.where(first_col, edge, current[:, :KP])
    current = lax.dynamic_update_slice(current, merged, (0, 0))
    global_cols = col * local_cols + jnp.arange(local_cols, dtype=jnp.int32)
    upper_mask = (global_rows[:, None] < KP) & (global_cols[None, :] > global_rows[:, None])
    return jnp.where(upper_mask, 0.0, current)


def solution(mesh):
    return jax.shard_map(
        local,
        mesh=mesh,
        in_specs=(
            P("sub", "row", "col"),
            P("sub", "row", "col"),
            P("sub", "col", None),
            P(),
            P(PLANE, "col"),
            P(PLANE, "col"),
        ),
        out_specs=P(PLANE, "col"),
        check_vma=False,
    )
```

```python
import functools

import jax
import jax.numpy as jnp
from jax import lax
from jax.experimental import pallas as pl
from jax.experimental.pallas import tpu as pltpu
from jax.sharding import PartitionSpec as P

BLK = 256
PSTEPS = 2
KP = PSTEPS * BLK
TILE = 128
HEADROOM = 14.0
PLANE = ("sub", "row")


high = lax.Precision.HIGH


def nt(a, b, precision=None):
    return lax.dot_general(
        a, b, (((1,), (1,)), ((), ())), precision=precision, preferred_element_type=jnp.float32
    )


def nn(a, b, precision=None):
    return lax.dot_general(
        a, b, (((1,), (0,)), ((), ())), precision=precision, preferred_element_type=jnp.float32
    )


def chip_bits():
    return [1 << b for b in range(1, lax.axis_size("row").bit_length() - 1)]


def row_pass(x, owner, cols, bits, done):
    rows, n = lax.axis_size("row"), lax.axis_size("col")
    away = lax.axis_index("row") ^ owner(lax.axis_index("col"))
    for bit in bits:
        pairs = []
        for c in cols:
            for d in range(rows):
                if d & ~done == 0:
                    pairs.append(((owner(c) ^ d) * n + c, (owner(c) ^ d ^ bit) * n + c))
        got = lax.ppermute(x, ("row", "col"), pairs)
        x = jnp.where((away & ~done) == 0, x, got)
        done |= bit
    return x


def line_blocks(units):
    n, col = lax.axis_size("col"), lax.axis_index("col")

    def side(t, up):
        if 2 * t < n:
            return units[t][0 if up else 1]
        keep = col >= t if up else col < t
        return jnp.where(keep, units[t][0], jnp.zeros_like(units[t][0]))

    out = [units[0][0]]
    for m in range(1, n):
        out.append(units[m][0] if 2 * m == n else side(m, True) + side(n - m, False))
    return out


def tree_stages(x):
    n = lax.axis_size("col")
    col = lax.axis_index("col")
    step = n // 2
    while step:
        got = lax.ppermute(x, "col", [(i, i + step) for i in range(0, n, 2 * step)])
        x = jnp.where(col & (2 * step - 1) == step, got, x)
        step //= 2
        yield x


def plane_stages(pieces, here):
    rows, subs = lax.axis_size("row"), lax.axis_size("sub")
    across = [rows << b for b in range(subs.bit_length() - 1)]
    along = chip_bits()
    orders = (along + across + [1], across + along + [1])
    done = [0, 0]
    for bits in zip(*orders):
        out = []
        for k, bit in enumerate(bits):
            pairs = [(d, d ^ bit) for d in range(rows * subs) if d & ~done[k] == 0]
            got = lax.ppermute(pieces[k], PLANE, pairs)
            out.append(jnp.where((here & ~done[k]) == 0, pieces[k], got))
            done[k] |= bit
        pieces = out
        yield pieces


def pack(x, power=None):
    if power is None:
        power = exponent(jnp.max(jnp.abs(x)))
    scaled = lax.pad(x * jnp.exp2(HEADROOM - power), power, [(0, 16, 0), (0, 0, 0)])
    return scaled.astype(jnp.float16)


def exponent(bound):
    return jnp.ceil(jnp.log2(jnp.maximum(bound, 1e-30)))


def powers(packed):
    return packed[-16:-15].astype(jnp.float32)


def unpack(packed):
    return packed[:-16].astype(jnp.float32) * jnp.exp2(powers(packed) - HEADROOM)


def split(x):
    top = x.astype(jnp.bfloat16)
    return top, (x - top.astype(jnp.float32)).astype(jnp.bfloat16)


def product(a, b, form):
    (a0, a1), (b0, b1) = split(a), split(b)
    return form(a0, b0) + (form(a0, b1) + form(a1, b0))


def eliminate(block):
    t = block.shape[0]
    lane = lax.broadcasted_iota(jnp.int32, (8, t), 1)
    sub = lax.broadcasted_iota(jnp.int32, (8, t), 0)
    rows = [block[8 * i : 8 * i + 8] for i in range(t // 8)]
    inverse = [jnp.where(lane == sub + 8 * i, 1.0, 0.0) for i in range(t // 8)]

    def wide(x):
        return jnp.broadcast_to(x, (8, t))

    for j in range(0, t, 2):
        q, p = divmod(j, 8)
        r1, r2 = wide(rows[q][p : p + 1]), wide(rows[q][p + 1 : p + 2])
        e1, e2 = wide(inverse[q][p : p + 1]), wide(inverse[q][p + 1 : p + 2])
        a, b, c = wide(r1[:, j : j + 1]), wide(r1[:, j + 1 : j + 2]), wide(r2[:, j + 1 : j + 2])
        over = 1.0 / a
        ratio = b * over
        under = 1.0 / (c - b * ratio)
        r2, e2 = r2 - ratio * r1, e2 - ratio * e1
        r1, e1, r2, e2 = r1 * over, e1 * over, r2 * under, e2 * under
        for i in range(q, t // 8):
            f1 = wide(rows[i][:, j : j + 1])
            f2 = wide(rows[i][:, j + 1 : j + 2]) - f1 * ratio
            if i == q:
                f1 = jnp.where(sub > p, f1, 0.0)
                f2 = jnp.where(sub > p + 1, f2, 0.0)
            rows[i] = rows[i] - f1 * r1 - f2 * r2
            inverse[i] = inverse[i] - f1 * e1 - f2 * e2
    return jnp.concatenate(rows, 0), jnp.concatenate(inverse, 0)


def factor_kernel(first, last, *refs):
    work_ref, lower_ref, inverse_ref = refs[-3:]
    size = work_ref.shape[0]
    if first == 0:
        work_ref[...] = refs[0][...]
        lower_ref[...] = jnp.zeros_like(lower_ref)
        inverse_ref[...] = jnp.zeros_like(inverse_ref)
    else:
        for source, target in zip(refs[:3], refs[3:]):
            target[...] = source[...]
    r = lax.broadcasted_iota(jnp.int32, (TILE, TILE), 0)
    c = lax.broadcasted_iota(jnp.int32, (TILE, TILE), 1)

    def step(b, carry):
        at = pl.multiple_of(b * TILE, TILE)
        here = pl.ds(at, TILE)
        upper, unit = eliminate(work_ref[here, here])
        pivots = jnp.sum(jnp.where(r == c, upper, 0.0), axis=1, keepdims=True)
        root = 1.0 / jnp.sqrt(pivots)
        diagonal = jnp.where(c >= r, upper * root, 0.0).T
        local = unit * root
        column = product(work_ref[:, here], local, nt)
        ids = lax.broadcasted_iota(jnp.int32, (size, TILE), 0)
        column = jnp.where(ids >= at + TILE, column, 0.0)
        work_ref[...] = work_ref[...] - product(column, column, nt)
        known = product(lower_ref[here, :], inverse_ref[...], nn)
        rr = lax.broadcasted_iota(jnp.int32, (TILE, size), 0)
        cc = lax.broadcasted_iota(jnp.int32, (TILE, size), 1)
        inverse_ref[here, :] = product(local, jnp.where(cc == rr + at, 1.0, 0.0) - known, nn)
        lower_ref[:, here] = column
        lower_ref[here, here] = diagonal
        return carry

    lax.fori_loop(first, last, step, 0)


def factor_steps(state, first, last):
    shape = jax.ShapeDtypeStruct(state[0].shape, jnp.float32)
    return pl.pallas_call(
        functools.partial(factor_kernel, first, last),
        out_shape=[shape] * 3,
        cost_estimate=pl.CostEstimate(
            flops=(last - first) * 10**10, transcendentals=0, bytes_accessed=3 * 2**21
        ),
        name="factor_pivot",
    )(*state)


def assemble_kernel(where_ref, pattern_ref, parent_ref, *refs):
    out_ref = refs[-1]
    i = pl.program_id(0)
    group_cols = parent_ref.shape[1] // BLK
    group_rows = pl.num_programs(0)
    for k in range(group_cols):
        cols = slice(k * BLK, (k + 1) * BLK)
        value = parent_ref[:, cols] * pattern_ref[i, k].astype(jnp.float32)
        for s, ref in enumerate(refs[:-1]):
            source = where_ref[s, group_rows + k]
            hit = jnp.logical_and(where_ref[s, i] >= 0, source >= 0)
            block = ref[:, pl.ds(pl.multiple_of(jnp.maximum(source, 0) * BLK, BLK), BLK)]
            value = value + jnp.where(hit, block, 0.0)
        out_ref[:, cols] = value


def assemble(places, pattern, parent, *children):
    rows, cols = parent.shape

    def source(s):
        shape = (BLK, children[s].shape[1])
        return pl.BlockSpec(shape, lambda i, w, p: (jnp.maximum(w[s, i], 0), 0))

    return pl.pallas_call(
        assemble_kernel,
        out_shape=jax.ShapeDtypeStruct(parent.shape, jnp.float32),
        grid_spec=pltpu.PrefetchScalarGridSpec(
            num_scalar_prefetch=2,
            grid=(rows // BLK,),
            in_specs=[pl.BlockSpec((BLK, cols), lambda i, w, p: (i, 0))]
            + [source(s) for s in range(len(children))],
            out_specs=pl.BlockSpec((BLK, cols), lambda i, w, p: (i, 0)),
        ),
        name="assemble",
    )(places, pattern, parent, *children)


def local(child_update, child_coupling, pivot_inverse, child_map, parent_front, block_pattern):
    update, coupling, inverse_rows = child_update[0], child_coupling[0], pivot_inverse[0]
    rows, width = update.shape
    full_depth = inverse_rows.shape[1]
    n, ranks = lax.axis_size("col"), lax.axis_size("row")
    col, row, sub = lax.axis_index("col"), lax.axis_index("row"), lax.axis_index("sub")
    here = sub * ranks + row
    local_rows, local_cols = parent_front.shape

    shift = (rows // width).bit_length() - 1
    owner = lambda c: c >> shift
    share = inverse_rows.shape[0] // ranks
    group_rows, group_cols = local_rows // BLK, local_cols // BLK
    child_rows, child_cols = rows // BLK, width // BLK
    home = (n - 1) // 2

    def place(first, count, targets):
        inside = lax.dynamic_slice_in_dim(child_map, first, count, 1)
        match = inside[:, None, :] == targets[None, :, None]
        return jnp.where(match.any(-1), jnp.argmax(match, axis=-1), -1).astype(jnp.int32)

    def slot(m):
        return jnp.where(col >= m, col - m, col - m + n)

    def in_order(blocks, axis):
        size = blocks[0].shape[axis]
        shape = tuple(d * (n if a == axis else 1) for a, d in enumerate(blocks[0].shape))
        out = jnp.zeros(shape, blocks[0].dtype)
        for m in sorted(range(len(blocks)), key=lambda m: max(m, n - m) if m else 0):
            out = lax.dynamic_update_slice_in_dim(out, blocks[m], slot(m) * size, axis)
        return out

    pivots = jnp.arange(PSTEPS)
    pivot_places = lax.dynamic_slice_in_dim(
        jnp.concatenate([place(0, child_rows, pivots), place(0, child_cols, pivots)], axis=1),
        sub, 1, 0,
    )
    base = jnp.where(here == 0, parent_front[:KP, :KP], 0.0)
    ones = jnp.where(here == 0, block_pattern[:PSTEPS, :PSTEPS], 1)
    pivot_update = assemble(pivot_places, ones, base, update)
    if home:
        pivot_update = lax.ppermute(pivot_update, ("row", "col"), [(0, home)])

    def slab(x):
        if width == rows:
            return x
        return lax.dynamic_slice_in_dim(x, col * width - (owner(col) << shift) * width, width, 0)

    mine = lax.dynamic_slice_in_dim(inverse_rows, row * share, share, 0)
    middle, part = full_depth // 2, share // 2
    given = lax.ppermute(mine[part:, middle:], "col", [(n - 1 - c, c) for c in range(n // 2)])
    right = jnp.where(col < n // 2, given, mine[:part, middle:])
    gathered = lax.all_gather(
        jnp.concatenate([mine[:, :middle], right], axis=0), ("col", "row"), axis=0, tiled=True
    ).reshape(n, ranks, share + part, middle)
    lefts = gathered[:, :, :share].reshape(full_depth, middle)
    halves = (gathered[n // 2 :, :, share:], gathered[: n // 2, :, share:][::-1])
    rights = jnp.concatenate(halves, axis=2).reshape(full_depth - middle, middle)
    inverse_low = lefts[:middle]
    inverse_high = jnp.concatenate([lefts[middle:], rights], axis=1)
    chips = chip_bits()
    units = {0: (coupling,)}
    ups = downs = coupling
    for t in range(1, n):
        ups = lax.ppermute(ups, "col", [(i, i + 1) for i in range(t - 1, n - 1)])
        downs = lax.ppermute(downs, "col", [(i + 1, i) for i in range(n - t)])
        now = {"line": [ups, downs]}
        if t == 2:
            now["lead"] = pivot_update
            now["top"] = jnp.max(jnp.abs(parent_front))
        if t == n - 1:
            now["inverse"] = (inverse_low, inverse_high)
        now = lax.optimization_barrier(now)
        if t == n - 1:
            inverse_low, inverse_high = now["inverse"]
        ups, downs = now["line"]
        units[t] = (ups, downs) if 2 * t < n else (ups + downs,)
        if t == 2:
            pivot_update, parent_top = now["lead"], now["top"]

    def along(x):
        return row_pass(slab(x), owner, range(n), chips, 0)

    def across(x):
        return row_pass(x, owner, range(n), [1], sum(chips))

    def panel_of(x):
        low = nt(x[:, :middle], inverse_low).astype(jnp.bfloat16)
        return low, nt(x, inverse_high).astype(jnp.bfloat16)

    def reduce_by(value, left, right):
        return value - (nt(left[0], right[0]) + nt(left[1], right[1]))

    row_panel = panel_of(in_order(line_blocks(units), 1))
    passed = [along(p) for p in row_panel]
    pivot_panel = []
    for part in row_panel:
        picked = []
        for i in range(PSTEPS):
            at = pivot_places[0, i]
            block = lax.dynamic_slice_in_dim(part, jnp.maximum(at, 0) * BLK, BLK, 0)
            picked.append(jnp.where(at >= 0, block, jnp.zeros_like(block)))
        pivot_panel.append(jnp.concatenate(picked, axis=0))
    sent = pack(reduce_by(pivot_update, pivot_panel, pivot_panel))
    pivot = jnp.where(col == home, sent, jnp.zeros_like(sent))
    for k in range(n):
        if k != home:
            pivot = pivot + lax.ppermute(sent, ("row", "col"), [(home, k)])
    pivot, passed[0] = lax.optimization_barrier((pivot, passed[0]))
    got = lax.ppermute(pivot, PLANE, [(0, ranks), (ranks, 0)])
    col_panel = [across(passed[0])]
    got, passed[1], col_panel[0] = lax.optimization_barrier((got, passed[1], col_panel[0]))
    col_panel.append(across(passed[1]))
    power = jnp.max(jnp.maximum(powers(pivot), powers(got))) + 1
    pivot = pack(unpack(pivot) + unpack(got), power)

    def onward(pivot, bits, done):
        for bit in bits:
            pairs = [
                (s * ranks + d, s * ranks + (d ^ bit))
                for s in range(2) for d in range(ranks) if d & ~done == 0
            ]
            got = lax.ppermute(pivot, PLANE, pairs)
            pivot = jnp.where((row & ~done) == 0, pivot, got)
            done |= bit
        return pivot

    pivot = onward(pivot, chips, 0)
    schur = reduce_by(update, row_panel, col_panel)
    pivot, schur = lax.optimization_barrier((pivot, schur))
    pivot = onward(pivot, [1], sum(chips))
    steps = KP // TILE
    state = factor_steps((unpack(pivot),), 0, steps // 2)

    half = rows // 2
    is_first = sub == 0
    upper, under = schur[:half], schur[half:]
    packed = [
        pack(jnp.where(is_first, upper, under)), pack(jnp.where(is_first, under, upper))
    ]
    straight = [(s * ranks + r, 2 * r + s) for s in range(2) for r in range(ranks)]
    crossed = [(s * ranks + r, 2 * r + 1 - s) for s in range(2) for r in range(ranks)]
    swap = [(i, i ^ 1) for i in range(2 * ranks)]
    got = lax.ppermute(packed[0], PLANE, straight)
    other = lax.ppermute(packed[1], PLANE, crossed)
    got, other, state = lax.optimization_barrier((got, other, state))
    pieces = [got, other] + [lax.ppermute(p, PLANE, swap) for p in (got, other)]
    core = here & 1
    child_of, half_of = (core, 1 - core, 1 - core, core), (core, core, 1 - core, 1 - core)
    row_places = place((here >> 1) * child_rows, child_rows, here * group_rows + jnp.arange(group_rows))
    col_places = place(col * child_cols, child_cols, col * group_cols + jnp.arange(group_cols))
    half_blocks = half // BLK
    places = []
    for s, h in zip(child_of, half_of):
        r = jnp.where(s == 0, row_places[0], row_places[1]) - h * half_blocks
        r = jnp.where((r >= 0) & (r < half_blocks), r, -1)
        places.append(jnp.concatenate([r, jnp.where(s == 0, col_places[0], col_places[1])]))
    highest = functools.reduce(jnp.maximum, [powers(p) for p in pieces])
    power = exponent(parent_top + 2 * jnp.exp2(jnp.max(highest)))
    current = assemble(jnp.stack(places), block_pattern, parent_front, *[unpack(p) for p in pieces])

    first_col = col == 0
    lead_stages = tree_stages(pack(current[:, :KP], power))
    raw_halves = [pack(current[: KP // 2], power), pack(current[KP // 2 : KP], power)]
    raw_stages = plane_stages(raw_halves, here)
    lead, raw_halves = next(lead_stages), next(raw_stages)
    state, raw_halves = lax.optimization_barrier((state, raw_halves))
    for lead in lead_stages:
        pass
    for raw_halves in raw_stages:
        pass
    lead = jnp.where(first_col, current[:, :KP], unpack(lead))
    raw = jnp.concatenate([unpack(p) for p in raw_halves], axis=0)
    _, lower, inverse = factor_steps(state, steps // 2, steps)
    global_rows = here * local_rows + jnp.arange(local_rows, dtype=jnp.int32)
    below = jnp.where((global_rows >= KP)[:, None], nt(lead, inverse, high), 0.0)
    current = current - nn(nn(below, inverse, high), raw, high)
    edge = jnp.concatenate([lower, jnp.zeros((local_rows - KP, KP), jnp.float32)], axis=0)
    edge = jnp.where((global_rows < KP)[:, None], edge, below)
    merged = jnp.where(first_col, edge, current[:, :KP])
    current = lax.dynamic_update_slice(current, merged, (0, 0))
    global_cols = col * local_cols + jnp.arange(local_cols, dtype=jnp.int32)
    upper_mask = (global_rows[:, None] < KP) & (global_cols[None, :] > global_rows[:, None])
    return jnp.where(upper_mask, 0.0, current)


def solution(mesh):
    return jax.shard_map(
        local,
        mesh=mesh,
        in_specs=(
            P("sub", "row", "col"),
            P("sub", "row", "col"),
            P("sub", "col", None),
            P(),
            P(PLANE, "col"),
            P(PLANE, "col"),
        ),
        out_specs=P(PLANE, "col"),
        check_vma=False,
    )
```
